32 devices in a mesh: dp: 4 (over z), adapter: 8 (over y, x, core).
Axes of the slice: x: 2, y: 2, z: 4, core: 2. Of those that a mesh axis runs over, the one named last changes fastest.
Arguments:
- states: bfloat16 [2, 1024, 8192], P(None, ('dp', 'adapter')), may hold values from -6 to 6
- request_slot_index: int32 [2, 1024, 1], P(None, ('dp', 'adapter')), may hold values from 0 to 7; in each aligned block of 32 rows (0 to 31, 32 to 63, ..., all dimensions but the last counted through in order) at most 8 rows name the same one
- down_weights: bfloat16 [32, 64, 8192], P(('dp', 'adapter')), may hold values from -0.0625 to 0.0625
- up_weights: bfloat16 [32, 64, 8192], P(('dp', 'adapter')), may hold values from -0.75 to 0.75
- active_adapter_owner: int32 [2, 8], replicated, may hold values from 0 to 3
Outputs:
- delta: bfloat16 [2, 1024, 8192], P(None, ('dp', 'adapter'))
The draws below stay inside these ranges and needn't reach their ends.
Inputs may be any that keep to these rules, and one draw needn't show every extreme that they name: `request_slot_index`: within the rows of one device at one step (aligned blocks of 32 rows), no column is named by more than 8 rows, a bound that some block reaches.
All inputs are finite; a program needn't handle non-finite values.
Results may differ from the reference program's by a relative error of at most 0.0049.
Values may be sent and summed in bfloat16 or wider, within the bound.
A program may use at most 64 MiB of HBM per device.

```python
import math
import jax
import jax.numpy as jnp
import numpy as np
from jax import lax

MODEL_DIM = 8192
ADAPTER_RANK = 64
ROWS_DEV = 32
STEPS = 2
COLS = 8
OWNERS = 4
CAP = 8
ROWS = 1024
ADAPTER_TOTAL = 32


def place_ends(values, rng, smallest, largest):
    place = [jax.random.randint(jax.random.fold_in(rng, axis), (), 0, length) for axis, length in enumerate(values.shape)]
    longest = values.shape.index(max(values.shape))
    neighbour = place[:longest] + [(place[longest] + 1) % values.shape[longest]] + place[longest + 1:]
    return values.at[tuple(place)].set(smallest).at[tuple(neighbour)].set(largest)


def level_of(rng, extent, shards, low, largest):
    loudness = 1.0
    for position, blocks in shards:
        draws = jax.random.uniform(jax.random.fold_in(jax.random.fold_in(rng, 6), position), (blocks,), jnp.float32, low / len(shards), largest / len(shards))
        loudness = loudness * jnp.repeat(jnp.exp(draws), extent[position] // blocks).reshape((-1,) + (1,) * (len(extent) - 1 - position))
    return loudness


def shared_out(rng, own, number, rows, count, top, limit, skew):
    sequence = jax.random.permutation(rng, count)
    heavy_load, common = load_shares(count, rows * top, limit, skew, True), load_shares(count, rows * top, limit, skew, False)
    places = jnp.arange(count)

    def named(sizes, rotation):
        used = int((sizes > 0).sum())
        fixed = max(1, used // 4)
        moved = fixed + (places - fixed + rotation * (used - fixed)) % max(1, count - fixed)
        return jnp.zeros((count,), jnp.int32).at[sequence[jnp.where(places < fixed, places, moved)]].set(jnp.asarray(sizes, jnp.int32))

    sizes = jnp.where(number % 4 == 0, named(heavy_load, number // 4), named(common, number - number // 4 - 1))
    mixed = jax.random.permutation(jax.random.fold_in(own, 3), count)
    donor, receiver = mixed[0:count // 2 * 2:2], mixed[1:count // 2 * 2:2]
    margin = jnp.minimum(sizes[donor] - 1, limit - sizes[receiver]) // 2
    margin = jnp.where((donor == sequence[0]) | (receiver == sequence[0]) | (sizes[receiver] == 0), 0, jnp.maximum(margin, 0))
    moved = jax.random.randint(jax.random.fold_in(own, 4), (count // 2,), 0, 1 << 20) % (margin + 1)
    sizes = sizes.at[donor].add(-moved).at[receiver].add(moved)
    members = jnp.searchsorted(jnp.cumsum(sizes), jnp.arange(rows * top), side="right").astype(jnp.int32)
    table = members.reshape(top, rows).T
    table = table[jax.random.permutation(jax.random.fold_in(own, 1), rows)]
    rotation = jax.random.randint(jax.random.fold_in(own, 2), (rows, 1), 0, top)
    return jnp.take_along_axis(table, (jnp.arange(top)[None, :] + rotation) % top, axis=1)


def load_shares(number_of, total, most, slope, full):
    loads = [(1 << 20) // math.isqrt(standing ** slope) + 1 for standing in range(1, number_of + 1)]
    largest = most if full else min(most, max(-(-total // number_of), total * loads[0] // sum(loads)))
    least = 1 if total - largest >= number_of - 1 else 0
    holding, surplus = [largest] + [least] * (number_of - 1), total - largest - least * (number_of - 1)
    while surplus > 0:
        candidates = [i for i in range(1, number_of) if holding[i] < largest] or [i for i in range(1, number_of) if holding[i] < most]
        pool, budget = sum([loads[i] for i in candidates]), surplus
        for i in candidates:
            extra = min(most - holding[i], max(1, budget * loads[i] // pool), surplus)
            holding[i] = holding[i] + extra
            surplus = surplus - extra
    return np.array(holding)


def noise(own_key, dims, width, bound, split=(), kind=jnp.bfloat16):
    values = width * jax.random.normal(own_key, dims, jnp.float32)
    if split:
        values = values * level_of(own_key, dims, split, -0.22, 0.18)
    return jnp.clip(values, -bound, bound).astype(kind)


def setup_inputs(seed: int = 0) -> dict:
    key_list = jax.random.split(jax.random.key(seed), 6)
    states = noise(key_list[0], (STEPS, ROWS, MODEL_DIM), 1.0, 6.0, ((1, 32),))
    request_slot_index_keys = jax.random.split(jax.random.fold_in(key_list[1], 1), STEPS * ROWS // ROWS_DEV)
    request_slot_index_turns = jax.random.permutation(jax.random.fold_in(key_list[1], 3), STEPS * ROWS // ROWS_DEV)
    request_slot_index = jax.vmap(lambda own, number: shared_out(jax.random.fold_in(key_list[1], 2), own, number, ROWS_DEV, COLS, 1, CAP, 2))(request_slot_index_keys, request_slot_index_turns).reshape((STEPS, ROWS, 1))
    down_weights = noise(key_list[2], (ADAPTER_TOTAL, ADAPTER_RANK, MODEL_DIM), MODEL_DIM ** -0.5, 0.0625, ((0, 32),))
    up_weights = noise(key_list[3], (ADAPTER_TOTAL, ADAPTER_RANK, MODEL_DIM), ADAPTER_RANK ** -0.5, 0.75, ((0, 32),))
    active_adapter_owner = place_ends(jax.random.randint(key_list[4], (STEPS, COLS), 0, OWNERS), jax.random.fold_in(key_list[4], 1), 0, OWNERS - 1).astype(jnp.int32)
    return dict(states=states, request_slot_index=request_slot_index, down_weights=down_weights, up_weights=up_weights, active_adapter_owner=active_adapter_owner)


def reference(states, request_slot_index, down_weights, up_weights, active_adapter_owner):
    most_rows = min(ROWS, (ROWS // ROWS_DEV) * CAP)
    per_step = []
    for step_index in range(STEPS):
        inputs = states[step_index]
        column_of_rows = request_slot_index[step_index, :, 0].astype(jnp.int32)

        def one_column(column):
            picked = jnp.argsort((column_of_rows != column).astype(jnp.int32), stable=True)[:most_rows].astype(jnp.int32)
            is_live = column_of_rows[picked] == column
            adapter_number = (active_adapter_owner[step_index, column] * COLS + column).astype(jnp.int32)
            down_weight_tile = lax.dynamic_index_in_dim(down_weights, adapter_number, 0, keepdims=False)
            up_weight_tile = lax.dynamic_index_in_dim(up_weights, adapter_number, 0, keepdims=False)
            chosen = inputs[picked]
            low_rank = lax.dot_general(chosen, down_weight_tile, (((1,), (1,)), ((), ())), preferred_element_type=jnp.float32).astype(jnp.bfloat16)
            result = jnp.dot(low_rank, up_weight_tile, preferred_element_type=jnp.float32).astype(jnp.bfloat16)
            result = jnp.where(is_live[:, None], result, jnp.zeros_like(result))
            return picked, result

        picked_all, results = lax.map(one_column, jnp.arange(COLS, dtype=jnp.int32))
        delta_rows = jnp.zeros((ROWS, MODEL_DIM), jnp.bfloat16).at[picked_all.reshape(-1)].add(results.reshape(-1, MODEL_DIM))
        per_step.append(delta_rows)
    return jnp.stack(per_step)
```

```python
import functools

import jax
import jax.numpy as jnp
from jax import lax
from jax.experimental import pallas as pl
from jax.experimental.pallas import tpu as pltpu
from jax.sharding import PartitionSpec as P

MESH = pl.DeviceIdType.MESH
F32 = jnp.float32
BF16 = jnp.bfloat16
WIDTH = 256
SKEW = 3
LAG = 3
GROUP = 2


def kernel(
    n, cols, steps, cap, block, wc, group,
    owner_ref, slot_ref, states_any, down_any, up_any, out_ref,
    states_ref, down_ref, up_ref, below, above, xout, arrived, dout, returned, low_acc, low, pack, unpack,
    in_sem, up_send, dn_send, x_send, d_send, below_sem, above_sem, x_sem, d_sem,
):
    z = lax.axis_index("dp")
    me = lax.axis_index("adapter")
    rows = states_any.shape[1]
    rank = down_any.shape[1]
    nw = states_any.shape[2] // wc
    nch = 2 * nw
    slots = cols * block
    not_first = z > 0
    not_last = z < n - 1

    pieces = nw // group
    pw = wc * group
    loads = [
        pltpu.make_async_copy(src, dst, in_sem.at[i])
        for i, (src, dst) in enumerate(
            ((down_any, down_ref), (up_any, up_ref), (states_any, states_ref))
        )
    ]
    for load in loads:
        load.start()

    def lanes(w):
        return pl.ds(pl.multiple_of(w * wc, wc), wc)

    def piece_lanes(p):
        return pl.ds(pl.multiple_of(p * pw, pw), pw)

    def block_rows(j):
        return pl.ds(pl.multiple_of(j * block, block), block)

    barrier = pltpu.get_barrier_semaphore()
    for o in range(1, cols):
        pl.semaphore_signal(
            barrier, inc=1, device_id={"adapter": lax.rem(me + o, cols)}, device_id_type=MESH
        )

    @pl.when(not_first)
    def _():
        pl.semaphore_signal(barrier, inc=1, device_id={"dp": z - 1}, device_id_type=MESH)

    @pl.when(not_last)
    def _():
        pl.semaphore_signal(barrier, inc=1, device_id={"dp": z + 1}, device_id_type=MESH)

    r_sub = lax.broadcasted_iota(jnp.int32, (rows, rows), 0)
    r_lane = lax.broadcasted_iota(jnp.int32, (rows, rows), 1)
    for s in range(steps):
        crow = slot_ref[s : s + 1, :]
        crow_b = jnp.broadcast_to(crow, (rows, rows))
        ccol = jnp.sum(jnp.where(r_sub == r_lane, crow_b, 0), axis=1, keepdims=True)
        same = jnp.broadcast_to(ccol, (rows, rows)) == crow_b
        rank_row = jnp.sum(jnp.where(same & (r_sub < r_lane), 1, 0), axis=0, keepdims=True)
        rank_col = jnp.sum(jnp.where(same & (r_lane < r_sub), 1, 0), axis=1, keepdims=True)
        trow = crow * block + s * cap + rank_row
        tcol = ccol * block + s * cap + rank_col
        pack[s] = jnp.where(
            lax.broadcasted_iota(jnp.int32, (slots, rows), 0) == trow, 1.0, 0.0
        ).astype(BF16)
        unpack[s] = jnp.where(
            lax.broadcasted_iota(jnp.int32, (rows, slots), 1) == tcol, 1.0, 0.0
        ).astype(BF16)
    low_acc[...] = jnp.zeros_like(low_acc)

    owners = [owner_ref[s, me] for s in range(steps)]
    for load in loads:
        load.wait()
    pl.semaphore_wait(
        barrier, cols - 1 + not_first.astype(jnp.int32) + not_last.astype(jnp.int32)
    )

    def own(k, use):
        @pl.when(k < nw)
        def _():
            use(down_ref[0, :, lanes(k)])

        @pl.when(k >= nw)
        def _():
            use(up_ref[0, :, lanes(k - nw)])

    def part(s):
        return pl.ds(s * rank, rank)

    def hop(buf, i, place, owner_places, target, recv_sem, send_sem):
        def copy(k, src, dst):
            return pltpu.make_async_remote_copy(
                src_ref=buf.at[k, src],
                dst_ref=buf.at[k, dst],
                send_sem=send_sem,
                recv_sem=recv_sem.at[k],
                device_id={"dp": target},
                device_id_type=MESH,
            )

        whole = pl.ds(0, steps * rank)
        second = i - SKEW
        later = i - SKEW * place

        @pl.when((place == 0) & (i < nch))
        def _():
            def use(mine):
                for s in range(steps):
                    buf[i, part(s), :] = mine

            own(i, use)
            copy(i, part(0), part(1)).start()

        @pl.when((place == 1) & (i < nch))
        def _():
            def use(mine):
                buf[i, part(0), :] = mine

            own(i, use)

            @pl.when(place < n - 1)
            def _():
                copy(i, part(0), part(0)).start()

        @pl.when((place == 1) & (second >= 0) & (second < nch))
        def _():
            copy(second, part(1), part(1)).wait_recv()

            @pl.when(place < n - 1)
            def _():
                copy(second, part(1), part(1)).start()

        @pl.when((place > 1) & (later >= 0) & (later < nch))
        def _():
            copy(later, whole, whole).wait_recv()

            def use(mine):
                theirs = [buf[later, part(s), :] for s in range(steps)]
                for s in range(steps):
                    value = theirs[s]
                    raw = place == 2
                    if s == 0:
                        value = lax.select_n(raw & (owner_places[s] == 0), value, theirs[1])
                    else:
                        value = lax.select_n(raw & (owner_places[s] == 0), value, theirs[1])
                        value = lax.select_n(raw & (owner_places[s] == 1), value, theirs[0])
                    buf[later, part(s), :] = lax.select_n(owner_places[s] == place, value, mine)

            own(later, use)

            @pl.when(place < n - 1)
            def _():
                copy(later, whole, whole).start()

    def wait_sent(buf, place, send_sem):
        @pl.when(place == 0)
        def _():
            sent = buf.at[:, part(0)]
            pltpu.make_async_copy(sent, sent, send_sem).wait()

        @pl.when((place > 0) & (place < n - 1))
        def _():
            pltpu.make_async_copy(buf, buf, send_sem).wait()

    partners = []
    for o in range(cols - 1, 0, -1):
        peer, bit = 0, 1
        while bit < cols:
            peer = peer + bit * lax.rem(lax.rem(me // bit, 2) + o // bit % 2, 2)
            bit = 2 * bit
        partners.append(peer if bit == cols else lax.rem(me + o, cols))

    def exchange(src, dst, w, span, send_sem, recv_sem):
        for peer in partners:
            pltpu.make_async_remote_copy(
                src_ref=src.at[w, block_rows(peer), span],
                dst_ref=dst.at[w, block_rows(me), span],
                send_sem=send_sem,
                recv_sem=recv_sem.at[w],
                device_id={"adapter": peer},
                device_id_type=MESH,
            ).start()
        dst[w, block_rows(me), span] = src[w, block_rows(me), span]

    def wait_exchange(dst, w, recv_sem):
        remote = dst.at[w, pl.ds(0, slots - block)]
        pltpu.make_async_copy(remote, remote, recv_sem.at[w]).wait()

    ups = owners
    dns = [n - 1 - owner for owner in owners]

    def pick(buf, k, place, owner_places, s):
        other = (place == 1) & (owner_places[s] == (0 if s == 0 else 1))
        return lax.select_n(other, buf[k, part(s), :], buf[k, part(1 if s == 0 else 0), :])

    def chosen(k):
        parts = []
        for s in range(steps):
            parts.append(
                lax.select_n(
                    owners[s] <= z,
                    pick(above, k, n - 1 - z, dns, s),
                    pick(below, k, z, ups, s),
                )
            )
        return jnp.concatenate(parts, axis=0)

    def iteration(i, carry):
        hop(below, i, z, ups, lax.rem(z + 1, n), below_sem, up_send)
        hop(above, i, n - 1 - z, dns, lax.rem(z + n - 1, n), above_sem, dn_send)

        @pl.when((lax.rem(i, group) == 0) & (i < nw))
        def _():
            p = i // group
            total = jnp.zeros((slots, pw), F32)
            for s in range(steps):
                total = total + jnp.dot(
                    pack[s], states_ref[s, :, piece_lanes(p)], preferred_element_type=F32
                )
            xout[p] = total.astype(BF16)
            exchange(xout, arrived, p, pl.ds(0, pw), x_send, x_sem)

        k = i - SKEW * (n - 1)

        @pl.when((k >= 0) & (k < nw) & (lax.rem(k, group) == 0))
        def _():
            wait_exchange(arrived, k // group, x_sem)

        @pl.when((k >= 0) & (k < nw))
        def _():
            low_acc[...] += lax.dot_general(
                arrived[k // group, :, lanes(lax.rem(k, group))],
                chosen(k),
                (((1,), (1,)), ((), ())),
                preferred_element_type=F32,
            )

        @pl.when(k == nw - 1)
        def _():
            of_row = lax.rem(lax.broadcasted_iota(jnp.int32, low.shape, 0), block) // cap
            of_col = lax.broadcasted_iota(jnp.int32, low.shape, 1) // rank
            low[...] = jnp.where(of_row == of_col, low_acc[...], 0.0).astype(BF16)

        @pl.when((k >= nw) & (k < nch))
        def _():
            w = k - nw
            dout[w // group, :, lanes(lax.rem(w, group))] = jnp.dot(
                low[...], chosen(k), preferred_element_type=F32
            ).astype(BF16)

        @pl.when((k >= nw) & (k < nch - group) & (lax.rem(k - nw, group) == group - 1))
        def _():
            exchange(dout, returned, (k - nw) // group, pl.ds(0, pw), d_send, d_sem)

        @pl.when((k >= nch - group) & (k < nch))
        def _():
            span = lanes(lax.rem(k - nw, group))
            exchange(dout, returned, pieces - 1, span, d_send, d_sem)

        w_out = k - nw - LAG

        @pl.when((w_out >= 0) & (w_out < nw) & (lax.rem(w_out, group) == group - 1))
        def _():
            p = w_out // group
            wait_exchange(returned, p, d_sem)
            for s in range(steps):
                out_ref[s, :, piece_lanes(p)] = jnp.dot(
                    unpack[s], returned[p], preferred_element_type=F32
                ).astype(BF16)

        return carry

    lax.fori_loop(0, nch + SKEW * (n - 1) + LAG, iteration, 0)

    wait_sent(below, z, up_send)
    wait_sent(above, n - 1 - z, dn_send)
    for buf, sem in ((xout, x_send), (dout, d_send)):
        sent = buf.at[:, pl.ds(0, slots - block)]
        pltpu.make_async_copy(sent, sent, sem).wait()


def body(n, cols, states, request_slot_index, down_weights, up_weights, active_adapter_owner):
    steps, rows, width = states.shape
    rank = down_weights.shape[1]
    cap = max(2, 2 * rows // cols)
    block = -(-steps * cap // 16) * 16
    slots = cols * block
    wc = min(WIDTH, width)
    nw = width // wc
    group = GROUP if nw % GROUP == 0 else 1
    vmem = pl.BlockSpec(memory_space=pltpu.VMEM)
    hbm = pl.BlockSpec(memory_space=pl.ANY)
    dma = pltpu.SemaphoreType.DMA
    stream = pltpu.VMEM((2 * nw, steps * rank, wc), BF16)
    piece = pltpu.VMEM((nw // group, slots, wc * group), BF16)
    return pl.pallas_call(
        functools.partial(kernel, n, cols, steps, cap, block, wc, group),
        out_shape=pltpu.VMEM(states.shape, states.dtype),
        in_specs=[pl.BlockSpec(memory_space=pltpu.SMEM), vmem, hbm, hbm, hbm],
        out_specs=vmem,
        scratch_shapes=[
            pltpu.VMEM(states.shape, BF16),
            pltpu.VMEM(down_weights.shape, BF16),
            pltpu.VMEM(up_weights.shape, BF16),
            stream, stream, piece, piece, piece, piece,
            pltpu.VMEM((slots, steps * rank), F32),
            pltpu.VMEM((slots, steps * rank), BF16),
            pltpu.VMEM((steps, slots, rows), BF16),
            pltpu.VMEM((steps, rows, slots), BF16),
            dma((3,)), dma, dma, dma, dma,
            dma((2 * nw,)), dma((2 * nw,)), dma((nw // group,)), dma((nw // group,)),
        ],
        compiler_params=pltpu.CompilerParams(
            collective_id=0, has_side_effects=True, vmem_limit_bytes=56 * 1024 * 1024
        ),
    )(active_adapter_owner, request_slot_index[:, :, 0], states, down_weights, up_weights)


TOKEN_CHUNKS = 16
EARLY = 2
PAIR = 2
TO_MID, FROM_MID, FROM_IN = 2, 5, 8
OUT_LAG = 3


def split_kernel(
    cols, steps, cap, wc, nt, early,
    owner_ref, slot_ref, states_any, down_any, up_any, out_ref,
    states_ref, dt, wcat, raw, u_out, v_out, u_in, v_in, m_out, inb, fin,
    xt_out, xt_in, xw_out, xw_in, dout, returned,
    acc, low_acc, low, lm_out, lm_in, lo_out, lo_in, pack_t, pack_w, unpack,
    in_sem, raw_send, u_send, v_send, m_send, f_send, xt_send, xw_send, d_send, lm_send, lo_send,
    raw_sem, u_sem, v_sem, in_pos, xt_sem, xw_sem, d_sem, lm_sem, lo_sem,
):
    z = lax.axis_index("dp")
    me = lax.axis_index("adapter")
    rows, width = states_any.shape[1:]
    rank = down_any.shape[1]
    block = steps * cap
    slots = cols * block
    half = wc // 2
    nc = width // wc
    nw = nc - nt
    npos = nw + nc
    pw = PAIR * wc
    nd = nc // PAIR
    low_tick = early + 2 * nt + FROM_MID - 1
    done_tick = low_tick + 2
    delta_tick = max(done_tick, early + nw + nc - nd + FROM_IN)
    plow_tick = early + FROM_IN + nt // 2
    xw_tick = nt // PAIR

    far = z // 2
    is_outer = (z == 0) | (z == 3)
    is_inner = (z == 1) | (z == 2)
    inner_z = 1 + far
    outer_z = 3 * far
    mid_z = 2 - far

    owners = [owner_ref[s, me] for s in range(steps)]
    by_in = [a == inner_z for a in owners]
    by_out = [a == outer_z for a in owners]
    mine = [i | o for i, o in zip(by_in, by_out)]
    any_out = by_out[0] | by_out[1]

    def lanes(k, n):
        return pl.ds(pl.multiple_of(k * n, n), n)

    def block_rows(j):
        return pl.ds(pl.multiple_of(j * block, block), block)

    tw = nt * wc
    loads = [
        pltpu.make_async_copy(src, dst, in_sem.at[i])
        for i, (src, dst) in enumerate(
            (
                (states_any, states_ref),
                (up_any.at[0], wcat.at[:, pl.ds(nw * wc, width)]),
                (down_any.at[0, :, pl.ds(tw, nw * wc)], wcat.at[:, pl.ds(0, nw * wc)]),
                (down_any.at[0, :, pl.ds(0, tw)], dt),
            )
        )
    ]
    for load in loads:
        load.start()

    barrier = pltpu.get_barrier_semaphore()
    for o in range(1, cols):
        pl.semaphore_signal(
            barrier, inc=1, device_id={"adapter": lax.rem(me + o, cols)}, device_id_type=MESH
        )

    @pl.when(z > 0)
    def _():
        pl.semaphore_signal(barrier, inc=1, device_id={"dp": z - 1}, device_id_type=MESH)

    @pl.when(z < 3)
    def _():
        pl.semaphore_signal(barrier, inc=1, device_id={"dp": z + 1}, device_id_type=MESH)

    r_sub = lax.broadcasted_iota(jnp.int32, (rows, rows), 0)
    r_lane = lax.broadcasted_iota(jnp.int32, (rows, rows), 1)
    for s in range(steps):
        crow = slot_ref[s : s + 1, :]
        crow_b = jnp.broadcast_to(crow, (rows, rows))
        ccol = jnp.sum(jnp.where(r_sub == r_lane, crow_b, 0), axis=1, keepdims=True)
        same = jnp.broadcast_to(ccol, (rows, rows)) == crow_b
        rank_row = jnp.sum(jnp.where(same & (r_sub < r_lane), 1, 0), axis=0, keepdims=True)
        rank_col = jnp.sum(jnp.where(same & (r_lane < r_sub), 1, 0), axis=1, keepdims=True)
        at = lax.broadcasted_iota(jnp.int32, (slots, rows), 0)
        for g in range(2):
            pack_t[s, g] = jnp.where(at == crow * block + g * cap + rank_row, 1.0, 0.0).astype(BF16)
        pack_w[s] = jnp.where(at == crow * block + s * cap + rank_row, 1.0, 0.0).astype(BF16)
        unpack[s] = jnp.where(
            lax.broadcasted_iota(jnp.int32, (rows, slots), 1) == ccol * block + s * cap + rank_col,
            1.0,
            0.0,
        ).astype(BF16)
    low_acc[...] = jnp.zeros_like(low_acc)
    acc[...] = jnp.zeros_like(acc)

    for load in loads:
        load.wait()
    pl.semaphore_wait(barrier, cols - 1 + (z > 0).astype(jnp.int32) + (z < 3).astype(jnp.int32))

    partners = []
    for o in range(cols - 1, 0, -1):
        peer, bit = 0, 1
        while bit < cols:
            peer = peer + bit * lax.rem(lax.rem(me // bit, 2) + o // bit % 2, 2)
            bit = 2 * bit
        partners.append(peer if bit == cols else lax.rem(me + o, cols))

    def exchange(src, dst, w, span, send_sem, recv_sem):
        for peer in partners:
            pltpu.make_async_remote_copy(
                src_ref=src.at[w, block_rows(peer), span],
                dst_ref=dst.at[w, block_rows(me), span],
                send_sem=send_sem,
                recv_sem=recv_sem.at[w],
                device_id={"adapter": peer},
                device_id_type=MESH,
            ).start()
        dst[w, block_rows(me), span] = src[w, block_rows(me), span]

    def wait_exchange(dst, w, recv_sem):
        remote = dst.at[w, pl.ds(0, slots - block)]
        pltpu.make_async_copy(remote, remote, recv_sem.at[w]).wait()

    def along(src, dst, target, send_sem, recv_sem):
        return pltpu.make_async_remote_copy(
            src_ref=src,
            dst_ref=dst,
            send_sem=send_sem,
            recv_sem=recv_sem,
            device_id={"dp": target},
            device_id_type=MESH,
        )

    def folded(x):
        return jnp.concatenate([x[:, :half], x[:, half:]], axis=0)

    def unfolded(x):
        return jnp.concatenate([x[:rank], x[rank:]], axis=1)

    def across(a, b):
        return lax.dot_general(a, b, (((1,), (1,)), ((), ())), preferred_element_type=F32)

    def token(t, s):
        return xt_in[t // PAIR, :, lanes(s * PAIR + lax.rem(t, PAIR), half)]

    def chunk_at(p):
        return lax.rem(p + npos - early, npos)

    def both(p):
        return jnp.concatenate([unfolded(fin[p, s]) for s in range(steps)], axis=0)

    def known(w):
        own = folded(wcat[:, lanes(w, wc)])
        theirs = folded(raw[:, lanes(w, wc)])
        return [lax.select_n(by_in[s], theirs, own) for s in range(steps)]

    def iteration(i, carry):
        @pl.when(i < nt // PAIR)
        def _():
            for s in range(steps):
                packs = jnp.concatenate([pack_t[s, g] for g in range(2)], axis=1)
                parts = []
                for c in range(PAIR):
                    wide = states_ref[s, :, lanes(i * PAIR + c, wc)]
                    parts.append(jnp.concatenate([wide[:, :half], wide[:, half:]], axis=0))
                xt_out[i, :, pl.ds(s * PAIR * half, PAIR * half)] = jnp.dot(
                    packs, jnp.concatenate(parts, axis=1), preferred_element_type=F32
                ).astype(BF16)
            exchange(xt_out, xt_in, i, pl.ds(0, pw), xt_send, xt_sem)

        a = i - xw_tick

        @pl.when((a >= 0) & (a < nw // PAIR))
        def _():
            packs = jnp.concatenate([pack_w[s] for s in range(steps)], axis=1)
            wide = jnp.concatenate(
                [states_ref[s, :, lanes(nt // PAIR + a, pw)] for s in range(steps)], axis=0
            )
            xw_out[a] = jnp.dot(packs, wide, preferred_element_type=F32).astype(BF16)
            exchange(xw_out, xw_in, a, pl.ds(0, pw), xw_send, xw_sem)

        @pl.when(is_outer & (i < npos))
        def _():
            w = chunk_at(i)
            along(
                wcat.at[:, lanes(w, wc)], raw.at[:, lanes(w, wc)], inner_z, raw_send, raw_sem.at[w]
            ).start()
            t = i - early

            @pl.when((t >= 0) & (t < nt))
            def _():
                @pl.when(lax.rem(t, PAIR) == 0)
                def _():
                    wait_exchange(xt_in, t // PAIR, xt_sem)

                mine_t = folded(dt[:, lanes(t, wc)])
                u_out[t] = lax.select_n(any_out, token(t, 0), mine_t)
                along(u_out.at[t], u_in.at[t], inner_z, u_send, u_sem.at[t]).start()
                v_out[t] = lax.select_n(by_out[1], token(t, 1), token(t, 0))
                for s in range(steps):
                    acc[0, s, 0:slots] += across(token(t, s), mine_t)

            @pl.when((t >= nt) & (t < 2 * nt))
            def _():
                along(v_out.at[t - nt], v_in.at[t - nt], inner_z, v_send, v_sem.at[t - nt]).start()

        p = i - TO_MID

        @pl.when(is_inner & (p >= 0) & (p < npos))
        def _():
            w = chunk_at(p)
            theirs = raw.at[:, lanes(w, wc)]
            along(theirs, theirs, inner_z, raw_send, raw_sem.at[w]).wait_recv()
            weights = known(w)
            t = p - early

            @pl.when((t < 0) | (t >= 2 * nt))
            def _():
                for s in range(steps):
                    m_out[p, s] = weights[s]

            @pl.when((t >= 0) & (t < nt))
            def _():
                @pl.when(lax.rem(t, PAIR) == 0)
                def _():
                    wait_exchange(xt_in, t // PAIR, xt_sem)

                for s in range(steps):
                    m_out[p, s] = lax.select_n(mine[s], token(t, s), weights[s])

            @pl.when((t >= nt) & (t < 2 * nt))
            def _():
                v = t - nt
                along(v_out.at[v], v_in.at[v], inner_z, v_send, v_sem.at[v]).wait_recv()
                first = lax.select_n(by_out[1], u_in[v], v_in[v])
                m_out[p, 0] = lax.select_n(mine[0], first, weights[0])
                m_out[p, 1] = lax.select_n(mine[1], v_in[v], weights[1])

            along(m_out.at[p], inb.at[p], mid_z, m_send, in_pos.at[p]).start()

        q = i - FROM_MID

        @pl.when(is_inner & (q >= 0) & (q < npos))
        def _():
            along(m_out.at[q], inb.at[q], mid_z, m_send, in_pos.at[q]).wait_recv()
            weights = known(chunk_at(q))
            for s in range(steps):
                fin[q, s] = lax.select_n(mine[s], inb[q, s], weights[s])
            along(fin.at[q], inb.at[q], outer_z, f_send, in_pos.at[q]).start()
            t = q - early

            @pl.when((t >= 0) & (t < nt))
            def _():
                along(u_out.at[t], u_in.at[t], inner_z, u_send, u_sem.at[t]).wait_recv()
                mine_t = folded(dt[:, lanes(t, wc)])
                for s in range(steps):
                    table = lax.select_n(by_out[s], mine_t, u_in[t])
                    given = jnp.concatenate([token(t, s), inb[q, s]], axis=0)
                    acc[0, s] += across(given, table)

            @pl.when((t >= nt) & (t < 2 * nt))
            def _():
                v = t - nt
                mine_t = folded(dt[:, lanes(v, wc)])
                for s in range(steps):
                    table = lax.select_n(by_out[s], mine_t, u_in[v])
                    theirs = v_in[v]
                    if s == 0:
                        theirs = lax.select_n(by_out[1], u_in[v], theirs)
                    given = jnp.concatenate([theirs, inb[q, s]], axis=0)
                    acc[1, s] += across(given, table)

        r = i - FROM_IN

        @pl.when(is_outer & (r >= 0) & (r < npos))
        def _():
            along(fin.at[r], inb.at[r], outer_z, f_send, in_pos.at[r]).wait_recv()
            own = folded(wcat[:, lanes(chunk_at(r), wc)])
            for s in range(steps):
                fin[r, s] = lax.select_n(by_out[s], inb[r, s], own)

        c = i - plow_tick

        @pl.when((c >= 0) & (c < nw))
        def _():
            @pl.when(lax.rem(c, PAIR) == 0)
            def _():
                wait_exchange(xw_in, c // PAIR, xw_sem)

            low_acc[...] += across(
                xw_in[c // PAIR, :, lanes(lax.rem(c, PAIR), wc)], both(early + c)
            )

        lane = lax.broadcasted_iota(jnp.int32, (cols * cap, steps * rank), 1)

        def per_step(flags):
            return jnp.where(lane < rank, flags[0].astype(jnp.int32), flags[1].astype(jnp.int32)) != 0

        def reduced(k, part):
            out = []
            for s in range(steps):
                x = acc[k, s, part * slots : (part + 1) * slots].reshape(cols, 2, cap, 2 * rank)
                x = [x[:, g].reshape(cols * cap, 2 * rank) for g in range(2)]
                x[1 - s] = pltpu.roll(x[1 - s], rank, axis=1)
                out.append(x[0] + x[1])
            return jnp.where(lane < rank, out[0], out[1])

        @pl.when(is_inner & (i == low_tick))
        def _():
            for k in range(2):
                lm_out[k] = reduced(k, 1)
            along(lm_out, lm_in, mid_z, lm_send, lm_sem).start()

        def finish(part):
            spread = jnp.broadcast_to(
                part.reshape(cols, 1, cap, steps * rank), (cols, steps, cap, steps * rank)
            ).reshape(slots, steps * rank)
            of_row = lax.rem(lax.broadcasted_iota(jnp.int32, low.shape, 0), block) // cap
            of_col = lax.broadcasted_iota(jnp.int32, low.shape, 1) // rank
            low[...] = jnp.where(of_row == of_col, low_acc[...] + spread, 0.0).astype(BF16)

        @pl.when(is_inner & (i == done_tick))
        def _():
            along(lm_out, lm_in, mid_z, lm_send, lm_sem).wait_recv()
            here = per_step(mine)
            lo_out[...] = jnp.where(here, reduced(1, 0), lm_in[1])
            along(lo_out, lo_in, outer_z, lo_send, lo_sem).start()
            finish(jnp.where(here, reduced(0, 0), lm_in[0]))

        @pl.when(is_outer & (i == done_tick))
        def _():
            along(lo_out, lo_in, outer_z, lo_send, lo_sem).wait_recv()
            finish(jnp.where(per_step(by_out), reduced(0, 0), lo_in[...]))

        d = i - delta_tick

        @pl.when((d >= 0) & (d < nd))
        def _():
            for c in range(PAIR):
                at = lax.rem(early + nw + d * PAIR + c, npos)
                dout[d, :, pl.ds(c * wc, wc)] = jnp.dot(
                    low[...], both(at), preferred_element_type=F32
                ).astype(BF16)
            exchange(dout, returned, d, pl.ds(0, pw), d_send, d_sem)

        e = d - OUT_LAG

        @pl.when((e >= 0) & (e < nd))
        def _():
            wait_exchange(returned, e, d_sem)
            for s in range(steps):
                out_ref[s, :, lanes(e, pw)] = jnp.dot(
                    unpack[s], returned[e], preferred_element_type=F32
                ).astype(BF16)

        return carry

    lax.fori_loop(0, delta_tick + nd + OUT_LAG, iteration, 0)

    @pl.when(is_outer)
    def _():
        for buf, sem in ((wcat, raw_send), (u_out, u_send), (v_out, v_send)):
            pltpu.make_async_copy(buf, buf, sem).wait()

    @pl.when(is_inner)
    def _():
        for buf, sem in ((m_out, m_send), (fin, f_send), (lm_out, lm_send), (lo_out, lo_send)):
            pltpu.make_async_copy(buf, buf, sem).wait()

    for buf, sem in ((xt_out, xt_send), (xw_out, xw_send), (dout, d_send)):
        sent = buf.at[:, pl.ds(0, slots - block)]
        pltpu.make_async_copy(sent, sent, sem).wait()


def split_body(cols, states, request_slot_index, down_weights, up_weights, active_adapter_owner):
    steps, rows, width = states.shape
    rank = down_weights.shape[1]
    cap = 2 * rows // cols
    slots = cols * steps * cap
    wc = WIDTH
    nc = width // wc
    nt = TOKEN_CHUNKS * nc // 32
    nw = nc - nt
    npos = nw + nc
    early = EARLY
    vmem = pl.BlockSpec(memory_space=pltpu.VMEM)
    hbm = pl.BlockSpec(memory_space=pl.ANY)
    dma = pltpu.SemaphoreType.DMA
    fold = (2 * rank, wc // 2)
    tokens = pltpu.VMEM((nt // PAIR, slots, PAIR * wc), BF16)
    others = pltpu.VMEM((nw // PAIR, slots, PAIR * wc), BF16)
    deltas = pltpu.VMEM((nc // PAIR, slots, PAIR * wc), BF16)
    side = pltpu.VMEM((nt, *fold), BF16)
    stream = pltpu.VMEM((npos, steps, *fold), BF16)
    line = pltpu.VMEM((rank, npos * wc), BF16)
    lows = pltpu.VMEM((cols * cap, steps * rank), F32)
    mids = pltpu.VMEM((2, cols * cap, steps * rank), F32)
    return pl.pallas_call(
        functools.partial(split_kernel, cols, steps, cap, wc, nt, early),
        out_shape=pltpu.VMEM(states.shape, states.dtype),
        in_specs=[pl.BlockSpec(memory_space=pltpu.SMEM), vmem, hbm, hbm, hbm],
        out_specs=vmem,
        scratch_shapes=[
            pltpu.VMEM(states.shape, BF16),
            pltpu.VMEM((rank, nt * wc), BF16),
            line, line, side, side, side, side, stream, stream, stream,
            tokens, tokens, others, others, deltas, deltas,
            pltpu.VMEM((2, steps, 2 * slots, 2 * rank), F32),
            pltpu.VMEM((slots, steps * rank), F32),
            pltpu.VMEM((slots, steps * rank), BF16),
            mids, mids, lows, lows,
            pltpu.VMEM((steps, 2, slots, rows), BF16),
            pltpu.VMEM((steps, slots, rows), BF16),
            pltpu.VMEM((steps, rows, slots), BF16),
            dma((4,)), dma, dma, dma, dma, dma, dma, dma, dma, dma, dma,
            dma((npos,)), dma((nt,)), dma((nt,)), dma((npos,)),
            dma((nt // PAIR,)), dma((nw // PAIR,)), dma((nc // PAIR,)), dma, dma,
        ],
        compiler_params=pltpu.CompilerParams(
            collective_id=0, has_side_effects=True, vmem_limit_bytes=56 * 1024 * 1024
        ),
    )(active_adapter_owner, request_slot_index[:, :, 0], states, down_weights, up_weights)


def routed(n, cols, states, request_slot_index, down_weights, up_weights, active_adapter_owner):
    steps, rows, width = states.shape
    cap = 2 * rows // cols
    paired = steps == 2 and cap == 8 and cols * cap == down_weights.shape[1]
    if n == 4 and paired and width % (8 * WIDTH) == 0:
        run = functools.partial(split_body, cols)
    else:
        run = functools.partial(body, n, cols)
    return run(states, request_slot_index, down_weights, up_weights, active_adapter_owner)


def solution(mesh):
    return jax.shard_map(
        functools.partial(routed, mesh.shape["dp"], mesh.shape["adapter"]),
        mesh=mesh,
        in_specs=(
            P(None, ("dp", "adapter"), None),
            P(None, ("dp", "adapter"), None),
            P(("dp", "adapter"), None, None),
            P(("dp", "adapter"), None, None),
            P(),
        ),
        out_specs=P(None, ("dp", "adapter"), None),
        check_vma=False,
    )
```

```python
import functools

import jax
import jax.numpy as jnp
from jax import lax
from jax.experimental import pallas as pl
from jax.experimental.pallas import tpu as pltpu
from jax.sharding import PartitionSpec as P

MESH = pl.DeviceIdType.MESH
F32 = jnp.float32
BF16 = jnp.bfloat16
WIDTH = 256
SKEW = 3
LAG = 3
GROUP = 2


def kernel(
    n, cols, steps, cap, block, wc, group,
    owner_ref, slot_ref, states_any, down_any, up_any, out_ref,
    states_ref, down_ref, up_ref, below, above, xout, arrived, dout, returned, low_acc, low, pack, unpack,
    in_sem, up_send, dn_send, x_send, d_send, below_sem, above_sem, x_sem, d_sem,
):
    z = lax.axis_index("dp")
    me = lax.axis_index("adapter")
    rows = states_any.shape[1]
    rank = down_any.shape[1]
    nw = states_any.shape[2] // wc
    nch = 2 * nw
    slots = cols * block
    not_first = z > 0
    not_last = z < n - 1

    pieces = nw // group
    pw = wc * group
    loads = [
        pltpu.make_async_copy(src, dst, in_sem.at[i])
        for i, (src, dst) in enumerate(
            ((down_any, down_ref), (up_any, up_ref), (states_any, states_ref))
        )
    ]
    for load in loads:
        load.start()

    def lanes(w):
        return pl.ds(pl.multiple_of(w * wc, wc), wc)

    def piece_lanes(p):
        return pl.ds(pl.multiple_of(p * pw, pw), pw)

    def block_rows(j):
        return pl.ds(pl.multiple_of(j * block, block), block)

    barrier = pltpu.get_barrier_semaphore()
    for o in range(1, cols):
        pl.semaphore_signal(
            barrier, inc=1, device_id={"adapter": lax.rem(me + o, cols)}, device_id_type=MESH
        )

    @pl.when(not_first)
    def _():
        pl.semaphore_signal(barrier, inc=1, device_id={"dp": z - 1}, device_id_type=MESH)

    @pl.when(not_last)
    def _():
        pl.semaphore_signal(barrier, inc=1, device_id={"dp": z + 1}, device_id_type=MESH)

    r_sub = lax.broadcasted_iota(jnp.int32, (rows, rows), 0)
    r_lane = lax.broadcasted_iota(jnp.int32, (rows, rows), 1)
    for s in range(steps):
        crow = slot_ref[s : s + 1, :]
        crow_b = jnp.broadcast_to(crow, (rows, rows))
        ccol = jnp.sum(jnp.where(r_sub == r_lane, crow_b, 0), axis=1, keepdims=True)
        same = jnp.broadcast_to(ccol, (rows, rows)) == crow_b
        rank_row = jnp.sum(jnp.where(same & (r_sub < r_lane), 1, 0), axis=0, keepdims=True)
        rank_col = jnp.sum(jnp.where(same & (r_lane < r_sub), 1, 0), axis=1, keepdims=True)
        trow = crow * block + s * cap + rank_row
        tcol = ccol * block + s * cap + rank_col
        pack[s] = jnp.where(
            lax.broadcasted_iota(jnp.int32, (slots, rows), 0) == trow, 1.0, 0.0
        ).astype(BF16)
        unpack[s] = jnp.where(
            lax.broadcasted_iota(jnp.int32, (rows, slots), 1) == tcol, 1.0, 0.0
        ).astype(BF16)
    low_acc[...] = jnp.zeros_like(low_acc)

    owners = [owner_ref[s, me] for s in range(steps)]
    for load in loads:
        load.wait()
    pl.semaphore_wait(
        barrier, cols - 1 + not_first.astype(jnp.int32) + not_last.astype(jnp.int32)
    )

    def own(k, use):
        @pl.when(k < nw)
        def _():
            use(down_ref[0, :, lanes(k)])

        @pl.when(k >= nw)
        def _():
            use(up_ref[0, :, lanes(k - nw)])

    def part(s):
        return pl.ds(s * rank, rank)

    def hop(buf, i, place, owner_places, target, recv_sem, send_sem):
        def copy(k, src, dst):
            return pltpu.make_async_remote_copy(
                src_ref=buf.at[k, src],
                dst_ref=buf.at[k, dst],
                send_sem=send_sem,
                recv_sem=recv_sem.at[k],
                device_id={"dp": target},
                device_id_type=MESH,
            )

        whole = pl.ds(0, steps * rank)
        second = i - SKEW
        later = i - SKEW * place

        @pl.when((place == 0) & (i < nch))
        def _():
            def use(mine):
                for s in range(steps):
                    buf[i, part(s), :] = mine

            own(i, use)
            copy(i, part(0), part(1)).start()

        @pl.when((place == 1) & (i < nch))
        def _():
            def use(mine):
                buf[i, part(0), :] = mine

            own(i, use)

            @pl.when(place < n - 1)
            def _():
                copy(i, part(0), part(0)).start()

        @pl.when((place == 1) & (second >= 0) & (second < nch))
        def _():
            copy(second, part(1), part(1)).wait_recv()

            @pl.when(place < n - 1)
            def _():
                copy(second, part(1), part(1)).start()

        @pl.when((place > 1) & (later >= 0) & (later < nch))
        def _():
            copy(later, whole, whole).wait_recv()

            def use(mine):
                theirs = [buf[later, part(s), :] for s in range(steps)]
                for s in range(steps):
                    value = theirs[s]
                    raw = place == 2
                    if s == 0:
                        value = lax.select_n(raw & (owner_places[s] == 0), value, theirs[1])
                    else:
                        value = lax.select_n(raw & (owner_places[s] == 0), value, theirs[1])
                        value = lax.select_n(raw & (owner_places[s] == 1), value, theirs[0])
                    buf[later, part(s), :] = lax.select_n(owner_places[s] == place, value, mine)

            own(later, use)

            @pl.when(place < n - 1)
            def _():
                copy(later, whole, whole).start()

    def wait_sent(buf, place, send_sem):
        @pl.when(place == 0)
        def _():
            sent = buf.at[:, part(0)]
            pltpu.make_async_copy(sent, sent, send_sem).wait()

        @pl.when((place > 0) & (place < n - 1))
        def _():
            pltpu.make_async_copy(buf, buf, send_sem).wait()

    partners = []
    for o in range(cols - 1, 0, -1):
        peer, bit = 0, 1
        while bit < cols:
            peer = peer + bit * lax.rem(lax.rem(me // bit, 2) + o // bit % 2, 2)
            bit = 2 * bit
        partners.append(peer if bit == cols else lax.rem(me + o, cols))

    def exchange(src, dst, w, span, send_sem, recv_sem):
        for peer in partners:
            pltpu.make_async_remote_copy(
                src_ref=src.at[w, block_rows(peer), span],
                dst_ref=dst.at[w, block_rows(me), span],
                send_sem=send_sem,
                recv_sem=recv_sem.at[w],
                device_id={"adapter": peer},
                device_id_type=MESH,
            ).start()
        dst[w, block_rows(me), span] = src[w, block_rows(me), span]

    def wait_exchange(dst, w, recv_sem):
        remote = dst.at[w, pl.ds(0, slots - block)]
        pltpu.make_async_copy(remote, remote, recv_sem.at[w]).wait()

    ups = owners
    dns = [n - 1 - owner for owner in owners]

    def pick(buf, k, place, owner_places, s):
        other = (place == 1) & (owner_places[s] == (0 if s == 0 else 1))
        return lax.select_n(other, buf[k, part(s), :], buf[k, part(1 if s == 0 else 0), :])

    def chosen(k):
        parts = []
        for s in range(steps):
            parts.append(
                lax.select_n(
                    owners[s] <= z,
                    pick(above, k, n - 1 - z, dns, s),
                    pick(below, k, z, ups, s),
                )
            )
        return jnp.concatenate(parts, axis=0)

    def iteration(i, carry):
        hop(below, i, z, ups, lax.rem(z + 1, n), below_sem, up_send)
        hop(above, i, n - 1 - z, dns, lax.rem(z + n - 1, n), above_sem, dn_send)

        @pl.when((lax.rem(i, group) == 0) & (i < nw))
        def _():
            p = i // group
            total = jnp.zeros((slots, pw), F32)
            for s in range(steps):
                total = total + jnp.dot(
                    pack[s], states_ref[s, :, piece_lanes(p)], preferred_element_type=F32
                )
            xout[p] = total.astype(BF16)
            exchange(xout, arrived, p, pl.ds(0, pw), x_send, x_sem)

        k = i - SKEW * (n - 1)

        @pl.when((k >= 0) & (k < nw) & (lax.rem(k, group) == 0))
        def _():
            wait_exchange(arrived, k // group, x_sem)

        @pl.when((k >= 0) & (k < nw))
        def _():
            low_acc[...] += lax.dot_general(
                arrived[k // group, :, lanes(lax.rem(k, group))],
                chosen(k),
                (((1,), (1,)), ((), ())),
                preferred_element_type=F32,
            )

        @pl.when(k == nw - 1)
        def _():
            of_row = lax.rem(lax.broadcasted_iota(jnp.int32, low.shape, 0), block) // cap
            of_col = lax.broadcasted_iota(jnp.int32, low.shape, 1) // rank
            low[...] = jnp.where(of_row == of_col, low_acc[...], 0.0).astype(BF16)

        @pl.when((k >= nw) & (k < nch))
        def _():
            w = k - nw
            dout[w // group, :, lanes(lax.rem(w, group))] = jnp.dot(
                low[...], chosen(k), preferred_element_type=F32
            ).astype(BF16)

        @pl.when((k >= nw) & (k < nch - group) & (lax.rem(k - nw, group) == group - 1))
        def _():
            exchange(dout, returned, (k - nw) // group, pl.ds(0, pw), d_send, d_sem)

        @pl.when((k >= nch - group) & (k < nch))
        def _():
            span = lanes(lax.rem(k - nw, group))
            exchange(dout, returned, pieces - 1, span, d_send, d_sem)

        w_out = k - nw - LAG

        @pl.when((w_out >= 0) & (w_out < nw) & (lax.rem(w_out, group) == group - 1))
        def _():
            p = w_out // group
            wait_exchange(returned, p, d_sem)
            for s in range(steps):
                out_ref[s, :, piece_lanes(p)] = jnp.dot(
                    unpack[s], returned[p], preferred_element_type=F32
                ).astype(BF16)

        return carry

    lax.fori_loop(0, nch + SKEW * (n - 1) + LAG, iteration, 0)

    wait_sent(below, z, up_send)
    wait_sent(above, n - 1 - z, dn_send)
    for buf, sem in ((xout, x_send), (dout, d_send)):
        sent = buf.at[:, pl.ds(0, slots - block)]
        pltpu.make_async_copy(sent, sent, sem).wait()


def body(n, cols, states, request_slot_index, down_weights, up_weights, active_adapter_owner):
    steps, rows, width = states.shape
    rank = down_weights.shape[1]
    cap = max(2, 2 * rows // cols)
    block = -(-steps * cap // 16) * 16
    slots = cols * block
    wc = min(WIDTH, width)
    nw = width // wc
    group = GROUP if nw % GROUP == 0 else 1
    vmem = pl.BlockSpec(memory_space=pltpu.VMEM)
    hbm = pl.BlockSpec(memory_space=pl.ANY)
    dma = pltpu.SemaphoreType.DMA
    stream = pltpu.VMEM((2 * nw, steps * rank, wc), BF16)
    piece = pltpu.VMEM((nw // group, slots, wc * group), BF16)
    return pl.pallas_call(
        functools.partial(kernel, n, cols, steps, cap, block, wc, group),
        out_shape=pltpu.VMEM(states.shape, states.dtype),
        in_specs=[pl.BlockSpec(memory_space=pltpu.SMEM), vmem, hbm, hbm, hbm],
        out_specs=vmem,
        scratch_shapes=[
            pltpu.VMEM(states.shape, BF16),
            pltpu.VMEM(down_weights.shape, BF16),
            pltpu.VMEM(up_weights.shape, BF16),
            stream, stream, piece, piece, piece, piece,
            pltpu.VMEM((slots, steps * rank), F32),
            pltpu.VMEM((slots, steps * rank), BF16),
            pltpu.VMEM((steps, slots, rows), BF16),
            pltpu.VMEM((steps, rows, slots), BF16),
            dma((3,)), dma, dma, dma, dma,
            dma((2 * nw,)), dma((2 * nw,)), dma((nw // group,)), dma((nw // group,)),
        ],
        compiler_params=pltpu.CompilerParams(
            collective_id=0, has_side_effects=True, vmem_limit_bytes=56 * 1024 * 1024
        ),
    )(active_adapter_owner, request_slot_index[:, :, 0], states, down_weights, up_weights)


TOKEN_CHUNKS = 14
EARLY = 4
PAIR = 2
TO_MID, FROM_MID, FROM_IN = 2, 5, 8
OUT_LAG = 6
DONE_IN, DONE_OUT = 4, 5


def split_kernel(
    cols, steps, cap, wc, nt, early,
    owner_ref, slot_ref, states_any, down_any, up_any, out_ref,
    states_ref, dt, wcat, raw, u_out, v_out, u_in, v_in, m_out, inb, fin,
    xt_out, xt_in, xw_out, xw_in, dout, returned,
    acc, low_acc, low, lm_out, lm_in, lo_in, pack_t, pack_w, unpack,
    in_sem, raw_send, u_send, v_send, m_send, f_send, xt_send, xw_send, d_send, lm_send,
    raw_sem, u_sem, v_sem, in_pos, xt_sem, xw_sem, d_sem, lm_sem, lo_sem,
):
    z = lax.axis_index("dp")
    me = lax.axis_index("adapter")
    rows, width = states_any.shape[1:]
    rank = down_any.shape[1]
    block = steps * cap
    slots = cols * block
    half = wc // 2
    nc = width // wc
    nw = nc - nt
    npos = nw + nc
    pw = PAIR * wc
    nd = nc // PAIR
    low_tick = early + 2 * nt + FROM_MID - 1
    roles = [(low_tick + DONE_IN, nw + FROM_MID), (low_tick + DONE_OUT, nw + FROM_IN)]
    bulks = [min(max(done - base, 0), nd) for done, base in roles]
    ends = [
        max(done + bulk, base + 2 * nd) if bulk < nd else done + bulk
        for (done, base), bulk in zip(roles, bulks)
    ]
    plow_tick = early + FROM_IN + nt // 2
    xw_tick = nt // PAIR

    far = z // 2
    is_outer = (z == 0) | (z == 3)
    is_inner = (z == 1) | (z == 2)
    inner_z = 1 + far
    outer_z = 3 * far
    mid_z = 2 - far
    across_z = jnp.where(is_inner, 3 - outer_z, 3 - inner_z)
    done_tick = jnp.where(is_inner, roles[0][0], roles[1][0])
    base_tick = jnp.where(is_inner, roles[0][1], roles[1][1])
    bulk = jnp.where(is_inner, bulks[0], bulks[1])

    owners = [owner_ref[s, me] for s in range(steps)]
    by_in = [a == inner_z for a in owners]
    by_out = [a == outer_z for a in owners]
    mine = [i | o for i, o in zip(by_in, by_out)]
    any_out = by_out[0] | by_out[1]

    def lanes(k, n):
        return pl.ds(pl.multiple_of(k * n, n), n)

    def block_rows(j):
        return pl.ds(pl.multiple_of(j * block, block), block)

    tw = nt * wc
    loads = [
        pltpu.make_async_copy(src, dst, in_sem.at[i])
        for i, (src, dst) in enumerate(
            (
                (states_any, states_ref),
                (up_any.at[0], wcat.at[:, pl.ds(nw * wc, width)]),
                (down_any.at[0, :, pl.ds(tw, nw * wc)], wcat.at[:, pl.ds(0, nw * wc)]),
                (down_any.at[0, :, pl.ds(0, tw)], dt),
            )
        )
    ]
    for load in loads:
        load.start()

    barrier = pltpu.get_barrier_semaphore()
    for o in range(1, cols):
        pl.semaphore_signal(
            barrier, inc=1, device_id={"adapter": lax.rem(me + o, cols)}, device_id_type=MESH
        )

    pl.semaphore_signal(barrier, inc=1, device_id={"dp": across_z}, device_id_type=MESH)

    @pl.when(z > 0)
    def _():
        pl.semaphore_signal(barrier, inc=1, device_id={"dp": z - 1}, device_id_type=MESH)

    @pl.when(z < 3)
    def _():
        pl.semaphore_signal(barrier, inc=1, device_id={"dp": z + 1}, device_id_type=MESH)

    r_sub = lax.broadcasted_iota(jnp.int32, (rows, rows), 0)
    r_lane = lax.broadcasted_iota(jnp.int32, (rows, rows), 1)
    for s in range(steps):
        crow = slot_ref[s : s + 1, :]
        crow_b = jnp.broadcast_to(crow, (rows, rows))
        ccol = jnp.sum(jnp.where(r_sub == r_lane, crow_b, 0), axis=1, keepdims=True)
        same = jnp.broadcast_to(ccol, (rows, rows)) == crow_b
        rank_row = jnp.sum(jnp.where(same & (r_sub < r_lane), 1, 0), axis=0, keepdims=True)
        rank_col = jnp.sum(jnp.where(same & (r_lane < r_sub), 1, 0), axis=1, keepdims=True)
        at = lax.broadcasted_iota(jnp.int32, (slots, rows), 0)
        for g in range(2):
            pack_t[s, g] = jnp.where(at == crow * block + g * cap + rank_row, 1.0, 0.0).astype(BF16)
        pack_w[s] = jnp.where(at == crow * block + s * cap + rank_row, 1.0, 0.0).astype(BF16)
        unpack[s] = jnp.where(
            lax.broadcasted_iota(jnp.int32, (rows, slots), 1) == ccol * block + s * cap + rank_col,
            1.0,
            0.0,
        ).astype(BF16)
    low_acc[...] = jnp.zeros_like(low_acc)
    acc[...] = jnp.zeros_like(acc)

    for load in loads:
        load.wait()
    pl.semaphore_wait(barrier, cols + (z > 0).astype(jnp.int32) + (z < 3).astype(jnp.int32))

    partners = []
    for o in range(cols - 1, 0, -1):
        peer, bit = 0, 1
        while bit < cols:
            peer = peer + bit * lax.rem(lax.rem(me // bit, 2) + o // bit % 2, 2)
            bit = 2 * bit
        partners.append(peer if bit == cols else lax.rem(me + o, cols))

    def exchange(src, dst, w, span, send_sem, recv_sem):
        for peer in partners:
            pltpu.make_async_remote_copy(
                src_ref=src.at[w, block_rows(peer), span],
                dst_ref=dst.at[w, block_rows(me), span],
                send_sem=send_sem,
                recv_sem=recv_sem.at[w],
                device_id={"adapter": peer},
                device_id_type=MESH,
            ).start()
        dst[w, block_rows(me), span] = src[w, block_rows(me), span]

    def wait_exchange(dst, w, recv_sem):
        remote = dst.at[w, pl.ds(0, slots - block)]
        pltpu.make_async_copy(remote, remote, recv_sem.at[w]).wait()

    def along(src, dst, target, send_sem, recv_sem):
        return pltpu.make_async_remote_copy(
            src_ref=src,
            dst_ref=dst,
            send_sem=send_sem,
            recv_sem=recv_sem,
            device_id={"dp": target},
            device_id_type=MESH,
        )

    def folded(x):
        return jnp.concatenate([x[:, :half], x[:, half:]], axis=0)

    def unfolded(x):
        return jnp.concatenate([x[:rank], x[rank:]], axis=1)

    def across(a, b):
        return lax.dot_general(a, b, (((1,), (1,)), ((), ())), preferred_element_type=F32)

    def token(t, s):
        return xt_in[t // PAIR, :, lanes(s * PAIR + lax.rem(t, PAIR), half)]

    def chunk_at(p):
        return lax.rem(p + npos - early, npos)

    def both(p):
        return jnp.concatenate([unfolded(fin[p, s]) for s in range(steps)], axis=0)

    def known(w):
        own = folded(wcat[:, lanes(w, wc)])
        theirs = folded(raw[:, lanes(w, wc)])
        return [lax.select_n(by_in[s], theirs, own) for s in range(steps)]

    def iteration(i, carry):
        @pl.when(is_outer & (i < npos))
        def _():
            w = chunk_at(i)
            along(
                wcat.at[:, lanes(w, wc)], raw.at[:, lanes(w, wc)], inner_z, raw_send, raw_sem.at[w]
            ).start()

        @pl.when(i < nt // PAIR)
        def _():
            for s in range(steps):
                packs = jnp.concatenate([pack_t[s, g] for g in range(2)], axis=1)
                parts = []
                for c in range(PAIR):
                    wide = states_ref[s, :, lanes(i * PAIR + c, wc)]
                    parts.append(jnp.concatenate([wide[:, :half], wide[:, half:]], axis=0))
                xt_out[i, :, pl.ds(s * PAIR * half, PAIR * half)] = jnp.dot(
                    packs, jnp.concatenate(parts, axis=1), preferred_element_type=F32
                ).astype(BF16)
            exchange(xt_out, xt_in, i, pl.ds(0, pw), xt_send, xt_sem)

        a = i - xw_tick

        @pl.when((a >= 0) & (a < nw // PAIR))
        def _():
            packs = jnp.concatenate([pack_w[s] for s in range(steps)], axis=1)
            wide = jnp.concatenate(
                [states_ref[s, :, lanes(nt // PAIR + a, pw)] for s in range(steps)], axis=0
            )
            xw_out[a] = jnp.dot(packs, wide, preferred_element_type=F32).astype(BF16)
            exchange(xw_out, xw_in, a, pl.ds(0, pw), xw_send, xw_sem)

        @pl.when(is_outer & (i < npos))
        def _():
            t = i - early

            @pl.when((t >= 0) & (t < nt))
            def _():
                @pl.when(lax.rem(t, PAIR) == 0)
                def _():
                    wait_exchange(xt_in, t // PAIR, xt_sem)

                mine_t = folded(dt[:, lanes(t, wc)])
                u_out[t] = lax.select_n(any_out, token(t, 0), mine_t)
                along(u_out.at[t], u_in.at[t], inner_z, u_send, u_sem.at[t]).start()
                v_out[t] = lax.select_n(by_out[1], token(t, 1), token(t, 0))
                for s in range(steps):
                    acc[0, s, 0:slots] += across(token(t, s), mine_t)

            @pl.when((t >= nt) & (t < 2 * nt))
            def _():
                along(v_out.at[t - nt], v_in.at[t - nt], inner_z, v_send, v_sem.at[t - nt]).start()

        p = i - TO_MID

        @pl.when(is_inner & (p >= 0) & (p < npos))
        def _():
            w = chunk_at(p)
            theirs = raw.at[:, lanes(w, wc)]
            along(theirs, theirs, inner_z, raw_send, raw_sem.at[w]).wait_recv()
            weights = known(w)
            t = p - early

            @pl.when((t < 0) | (t >= 2 * nt))
            def _():
                for s in range(steps):
                    m_out[p, s] = weights[s]

            @pl.when((t >= 0) & (t < nt))
            def _():
                @pl.when(lax.rem(t, PAIR) == 0)
                def _():
                    wait_exchange(xt_in, t // PAIR, xt_sem)

                for s in range(steps):
                    m_out[p, s] = lax.select_n(mine[s], token(t, s), weights[s])

            @pl.when((t >= nt) & (t < 2 * nt))
            def _():
                v = t - nt
                along(v_out.at[v], v_in.at[v], inner_z, v_send, v_sem.at[v]).wait_recv()
                first = lax.select_n(by_out[1], u_in[v], v_in[v])
                m_out[p, 0] = lax.select_n(mine[0], first, weights[0])
                m_out[p, 1] = lax.select_n(mine[1], v_in[v], weights[1])

            along(m_out.at[p], inb.at[p], mid_z, m_send, in_pos.at[p]).start()

        q = i - FROM_MID

        @pl.when(is_inner & (q >= 0) & (q < npos))
        def _():
            along(m_out.at[q], inb.at[q], mid_z, m_send, in_pos.at[q]).wait_recv()
            weights = known(chunk_at(q))
            for s in range(steps):
                fin[q, s] = lax.select_n(mine[s], inb[q, s], weights[s])
            along(fin.at[q], inb.at[q], outer_z, f_send, in_pos.at[q]).start()
            t = q - early

            @pl.when((t >= 0) & (t < nt))
            def _():
                along(u_out.at[t], u_in.at[t], inner_z, u_send, u_sem.at[t]).wait_recv()
                mine_t = folded(dt[:, lanes(t, wc)])
                for s in range(steps):
                    table = lax.select_n(by_out[s], mine_t, u_in[t])
                    given = jnp.concatenate([token(t, s), inb[q, s]], axis=0)
                    acc[0, s] += across(given, table)

            @pl.when((t >= nt) & (t < 2 * nt))
            def _():
                v = t - nt
                mine_t = folded(dt[:, lanes(v, wc)])
                for s in range(steps):
                    table = lax.select_n(by_out[s], mine_t, u_in[v])
                    theirs = v_in[v]
                    if s == 0:
                        theirs = lax.select_n(by_out[1], u_in[v], theirs)
                    given = jnp.concatenate([theirs, inb[q, s]], axis=0)
                    acc[1, s] += across(given, table)

        r = i - FROM_IN

        @pl.when(is_outer & (r >= 0) & (r < npos))
        def _():
            along(fin.at[r], inb.at[r], outer_z, f_send, in_pos.at[r]).wait_recv()
            own = folded(wcat[:, lanes(chunk_at(r), wc)])
            for s in range(steps):
                fin[r, s] = lax.select_n(by_out[s], inb[r, s], own)

        c = i - plow_tick

        @pl.when((c >= 0) & (c < nw))
        def _():
            @pl.when(lax.rem(c, PAIR) == 0)
            def _():
                wait_exchange(xw_in, c // PAIR, xw_sem)

            low_acc[...] += across(
                xw_in[c // PAIR, :, lanes(lax.rem(c, PAIR), wc)], both(early + c)
            )

        lane = lax.broadcasted_iota(jnp.int32, (cols * cap, steps * rank), 1)

        def per_step(flags):
            return jnp.where(lane < rank, flags[0].astype(jnp.int32), flags[1].astype(jnp.int32)) != 0

        def reduced(k, part):
            out = []
            for s in range(steps):
                x = acc[k, s, part * slots : (part + 1) * slots].reshape(cols, 2, cap, 2 * rank)
                x = [x[:, g].reshape(cols * cap, 2 * rank) for g in range(2)]
                x[1 - s] = pltpu.roll(x[1 - s], rank, axis=1)
                out.append(x[0] + x[1])
            return jnp.where(lane < rank, out[0], out[1])

        @pl.when(is_inner & (i == low_tick))
        def _():
            lm_out[0] = reduced(0, 1)
            lm_out[1] = reduced(1, 1)
            lm_out[2] = reduced(1, 0)
            along(lm_out.at[0], lm_in, mid_z, lm_send, lm_sem).start()
            along(lm_out.at[1], lo_in.at[1], across_z, lm_send, lo_sem.at[1]).start()
            along(lm_out.at[2], lo_in.at[0], outer_z, lm_send, lo_sem.at[0]).start()

        def finish(part):
            spread = jnp.broadcast_to(
                part.reshape(cols, 1, cap, steps * rank), (cols, steps, cap, steps * rank)
            ).reshape(slots, steps * rank)
            of_row = lax.rem(lax.broadcasted_iota(jnp.int32, low.shape, 0), block) // cap
            of_col = lax.broadcasted_iota(jnp.int32, low.shape, 1) // rank
            low[...] = jnp.where(of_row == of_col, low_acc[...] + spread, 0.0).astype(BF16)

        @pl.when(is_inner & (i == done_tick))
        def _():
            along(lm_out.at[0], lm_in, mid_z, lm_send, lm_sem).wait_recv()
            finish(jnp.where(per_step(mine), reduced(0, 0), lm_in[...]))

        @pl.when(is_outer & (i == done_tick))
        def _():
            for k in range(2):
                along(lm_out.at[2 - k], lo_in.at[k], outer_z, lm_send, lo_sem.at[k]).wait_recv()
            theirs = jnp.where(per_step(by_in), lo_in[0], lo_in[1])
            finish(jnp.where(per_step(by_out), reduced(0, 0), theirs))

        def place(v):
            return lax.rem(v + nd - early // PAIR, nd)

        def deltas(v, c):
            u = v * PAIR + c
            at = u + jnp.where(u < early, 0, nw)
            dout[place(v), :, lanes(c, wc)] = jnp.dot(
                low[...], both(at), preferred_element_type=F32
            ).astype(BF16)

        v = i - done_tick

        @pl.when((v >= 0) & (v < bulk))
        def _():
            for c in range(PAIR):
                deltas(v, c)
            exchange(dout, returned, place(v), pl.ds(0, pw), d_send, d_sem)

        n = i - base_tick

        @pl.when((n >= bulk * PAIR) & (n < nd * PAIR))
        def _():
            deltas(n // PAIR, lax.rem(n, PAIR))
            span = lanes(lax.rem(n, PAIR), wc)
            exchange(dout, returned, place(n // PAIR), span, d_send, d_sem)

        def gather(e):
            wait_exchange(returned, e, d_sem)
            for s in range(steps):
                out_ref[s, :, lanes(e, pw)] = jnp.dot(
                    unpack[s], returned[e], preferred_element_type=F32
                ).astype(BF16)

        v_back = v - OUT_LAG

        @pl.when((v_back >= 0) & (v_back < bulk))
        def _():
            gather(place(v_back))

        n_back = n - OUT_LAG - 1

        @pl.when((n_back >= bulk * PAIR) & (n_back < nd * PAIR) & (lax.rem(n_back, PAIR) == 0))
        def _():
            gather(place(n_back // PAIR))

        return carry

    lax.fori_loop(0, max(ends) + OUT_LAG + 1, iteration, 0)

    @pl.when(is_outer)
    def _():
        for buf, sem in ((wcat, raw_send), (u_out, u_send), (v_out, v_send)):
            pltpu.make_async_copy(buf, buf, sem).wait()

    @pl.when(is_inner)
    def _():
        for buf, sem in ((m_out, m_send), (fin, f_send), (lm_out, lm_send)):
            pltpu.make_async_copy(buf, buf, sem).wait()

    for buf, sem in ((xt_out, xt_send), (xw_out, xw_send), (dout, d_send)):
        sent = buf.at[:, pl.ds(0, slots - block)]
        pltpu.make_async_copy(sent, sent, sem).wait()


def split_body(cols, states, request_slot_index, down_weights, up_weights, active_adapter_owner):
    steps, rows, width = states.shape
    rank = down_weights.shape[1]
    cap = 2 * rows // cols
    slots = cols * steps * cap
    wc = WIDTH
    nc = width // wc
    nt = TOKEN_CHUNKS * nc // 32
    nw = nc - nt
    npos = nw + nc
    early = EARLY
    vmem = pl.BlockSpec(memory_space=pltpu.VMEM)
    hbm = pl.BlockSpec(memory_space=pl.ANY)
    dma = pltpu.SemaphoreType.DMA
    fold = (2 * rank, wc // 2)
    tokens = pltpu.VMEM((nt // PAIR, slots, PAIR * wc), BF16)
    others = pltpu.VMEM((nw // PAIR, slots, PAIR * wc), BF16)
    deltas = pltpu.VMEM((nc // PAIR, slots, PAIR * wc), BF16)
    side = pltpu.VMEM((nt, *fold), BF16)
    stream = pltpu.VMEM((npos, steps, *fold), BF16)
    line = pltpu.VMEM((rank, npos * wc), BF16)
    lows = (cols * cap, steps * rank)
    return pl.pallas_call(
        functools.partial(split_kernel, cols, steps, cap, wc, nt, early),
        out_shape=pltpu.VMEM(states.shape, states.dtype),
        in_specs=[pl.BlockSpec(memory_space=pltpu.SMEM), vmem, hbm, hbm, hbm],
        out_specs=vmem,
        scratch_shapes=[
            pltpu.VMEM(states.shape, BF16),
            pltpu.VMEM((rank, nt * wc), BF16),
            line, line, side, side, side, side, stream, stream, stream,
            tokens, tokens, others, others, deltas, deltas,
            pltpu.VMEM((2, steps, 2 * slots, 2 * rank), F32),
            pltpu.VMEM((slots, steps * rank), F32),
            pltpu.VMEM((slots, steps * rank), BF16),
            pltpu.VMEM((3, *lows), F32), pltpu.VMEM(lows, F32), pltpu.VMEM((2, *lows), F32),
            pltpu.VMEM((steps, 2, slots, rows), BF16),
            pltpu.VMEM((steps, slots, rows), BF16),
            pltpu.VMEM((steps, rows, slots), BF16),
            dma((4,)), dma, dma, dma, dma, dma, dma, dma, dma, dma,
            dma((npos,)), dma((nt,)), dma((nt,)), dma((npos,)),
            dma((nt // PAIR,)), dma((nw // PAIR,)), dma((nc // PAIR,)), dma, dma((2,)),
        ],
        compiler_params=pltpu.CompilerParams(
            collective_id=0, has_side_effects=True, vmem_limit_bytes=56 * 1024 * 1024
        ),
    )(active_adapter_owner, request_slot_index[:, :, 0], states, down_weights, up_weights)


def routed(n, cols, states, request_slot_index, down_weights, up_weights, active_adapter_owner):
    steps, rows, width = states.shape
    cap = 2 * rows // cols
    paired = steps == 2 and cap == 8 and cols * cap == down_weights.shape[1]
    if n == 4 and paired and width % (8 * WIDTH) == 0:
        run = functools.partial(split_body, cols)
    else:
        run = functools.partial(body, n, cols)
    return run(states, request_slot_index, down_weights, up_weights, active_adapter_owner)


def solution(mesh):
    return jax.shard_map(
        functools.partial(routed, mesh.shape["dp"], mesh.shape["adapter"]),
        mesh=mesh,
        in_specs=(
            P(None, ("dp", "adapter"), None),
            P(None, ("dp", "adapter"), None),
            P(("dp", "adapter"), None, None),
            P(("dp", "adapter"), None, None),
            P(),
        ),
        out_specs=P(None, ("dp", "adapter"), None),
        check_vma=False,
    )
```

```python
import functools

import jax
import jax.numpy as jnp
from jax import lax
from jax.experimental import pallas as pl
from jax.experimental.pallas import tpu as pltpu
from jax.sharding import PartitionSpec as P

MESH = pl.DeviceIdType.MESH
F32 = jnp.float32
BF16 = jnp.bfloat16
WIDTH = 256
SKEW = 3
LAG = 3
GROUP = 2


def kernel(
    n, cols, steps, cap, block, wc, group,
    owner_ref, slot_ref, states_any, down_any, up_any, out_ref,
    states_ref, down_ref, up_ref, below, above, xout, arrived, dout, returned, low_acc, low, pack, unpack,
    in_sem, up_send, dn_send, x_send, d_send, below_sem, above_sem, x_sem, d_sem,
):
    z = lax.axis_index("dp")
    me = lax.axis_index("adapter")
    rows = states_any.shape[1]
    rank = down_any.shape[1]
    nw = states_any.shape[2] // wc
    nch = 2 * nw
    slots = cols * block
    not_first = z > 0
    not_last = z < n - 1

    pieces = nw // group
    pw = wc * group
    loads = [
        pltpu.make_async_copy(src, dst, in_sem.at[i])
        for i, (src, dst) in enumerate(
            ((down_any, down_ref), (up_any, up_ref), (states_any, states_ref))
        )
    ]
    for load in loads:
        load.start()

    def lanes(w):
        return pl.ds(pl.multiple_of(w * wc, wc), wc)

    def piece_lanes(p):
        return pl.ds(pl.multiple_of(p * pw, pw), pw)

    def block_rows(j):
        return pl.ds(pl.multiple_of(j * block, block), block)

    barrier = pltpu.get_barrier_semaphore()
    for o in range(1, cols):
        pl.semaphore_signal(
            barrier, inc=1, device_id={"adapter": lax.rem(me + o, cols)}, device_id_type=MESH
        )

    @pl.when(not_first)
    def _():
        pl.semaphore_signal(barrier, inc=1, device_id={"dp": z - 1}, device_id_type=MESH)

    @pl.when(not_last)
    def _():
        pl.semaphore_signal(barrier, inc=1, device_id={"dp": z + 1}, device_id_type=MESH)

    r_sub = lax.broadcasted_iota(jnp.int32, (rows, rows), 0)
    r_lane = lax.broadcasted_iota(jnp.int32, (rows, rows), 1)
    for s in range(steps):
        crow = slot_ref[s : s + 1, :]
        crow_b = jnp.broadcast_to(crow, (rows, rows))
        ccol = jnp.sum(jnp.where(r_sub == r_lane, crow_b, 0), axis=1, keepdims=True)
        same = jnp.broadcast_to(ccol, (rows, rows)) == crow_b
        rank_row = jnp.sum(jnp.where(same & (r_sub < r_lane), 1, 0), axis=0, keepdims=True)
        rank_col = jnp.sum(jnp.where(same & (r_lane < r_sub), 1, 0), axis=1, keepdims=True)
        trow = crow * block + s * cap + rank_row
        tcol = ccol * block + s * cap + rank_col
        pack[s] = jnp.where(
            lax.broadcasted_iota(jnp.int32, (slots, rows), 0) == trow, 1.0, 0.0
        ).astype(BF16)
        unpack[s] = jnp.where(
            lax.broadcasted_iota(jnp.int32, (rows, slots), 1) == tcol, 1.0, 0.0
        ).astype(BF16)
    low_acc[...] = jnp.zeros_like(low_acc)

    owners = [owner_ref[s, me] for s in range(steps)]
    for load in loads:
        load.wait()
    pl.semaphore_wait(
        barrier, cols - 1 + not_first.astype(jnp.int32) + not_last.astype(jnp.int32)
    )

    def own(k, use):
        @pl.when(k < nw)
        def _():
            use(down_ref[0, :, lanes(k)])

        @pl.when(k >= nw)
        def _():
            use(up_ref[0, :, lanes(k - nw)])

    def part(s):
        return pl.ds(s * rank, rank)

    def hop(buf, i, place, owner_places, target, recv_sem, send_sem):
        def copy(k, src, dst):
            return pltpu.make_async_remote_copy(
                src_ref=buf.at[k, src],
                dst_ref=buf.at[k, dst],
                send_sem=send_sem,
                recv_sem=recv_sem.at[k],
                device_id={"dp": target},
                device_id_type=MESH,
            )

        whole = pl.ds(0, steps * rank)
        second = i - SKEW
        later = i - SKEW * place

        @pl.when((place == 0) & (i < nch))
        def _():
            def use(mine):
                for s in range(steps):
                    buf[i, part(s), :] = mine

            own(i, use)
            copy(i, part(0), part(1)).start()

        @pl.when((place == 1) & (i < nch))
        def _():
            def use(mine):
                buf[i, part(0), :] = mine

            own(i, use)

            @pl.when(place < n - 1)
            def _():
                copy(i, part(0), part(0)).start()

        @pl.when((place == 1) & (second >= 0) & (second < nch))
        def _():
            copy(second, part(1), part(1)).wait_recv()

            @pl.when(place < n - 1)
            def _():
                copy(second, part(1), part(1)).start()

        @pl.when((place > 1) & (later >= 0) & (later < nch))
        def _():
            copy(later, whole, whole).wait_recv()

            def use(mine):
                theirs = [buf[later, part(s), :] for s in range(steps)]
                for s in range(steps):
                    value = theirs[s]
                    raw = place == 2
                    if s == 0:
                        value = lax.select_n(raw & (owner_places[s] == 0), value, theirs[1])
                    else:
                        value = lax.select_n(raw & (owner_places[s] == 0), value, theirs[1])
                        value = lax.select_n(raw & (owner_places[s] == 1), value, theirs[0])
                    buf[later, part(s), :] = lax.select_n(owner_places[s] == place, value, mine)

            own(later, use)

            @pl.when(place < n - 1)
            def _():
                copy(later, whole, whole).start()

    def wait_sent(buf, place, send_sem):
        @pl.when(place == 0)
        def _():
            sent = buf.at[:, part(0)]
            pltpu.make_async_copy(sent, sent, send_sem).wait()

        @pl.when((place > 0) & (place < n - 1))
        def _():
            pltpu.make_async_copy(buf, buf, send_sem).wait()

    partners = []
    for o in range(cols - 1, 0, -1):
        peer, bit = 0, 1
        while bit < cols:
            peer = peer + bit * lax.rem(lax.rem(me // bit, 2) + o // bit % 2, 2)
            bit = 2 * bit
        partners.append(peer if bit == cols else lax.rem(me + o, cols))

    def exchange(src, dst, w, span, send_sem, recv_sem):
        for peer in partners:
            pltpu.make_async_remote_copy(
                src_ref=src.at[w, block_rows(peer), span],
                dst_ref=dst.at[w, block_rows(me), span],
                send_sem=send_sem,
                recv_sem=recv_sem.at[w],
                device_id={"adapter": peer},
                device_id_type=MESH,
            ).start()
        dst[w, block_rows(me), span] = src[w, block_rows(me), span]

    def wait_exchange(dst, w, recv_sem):
        remote = dst.at[w, pl.ds(0, slots - block)]
        pltpu.make_async_copy(remote, remote, recv_sem.at[w]).wait()

    ups = owners
    dns = [n - 1 - owner for owner in owners]

    def pick(buf, k, place, owner_places, s):
        other = (place == 1) & (owner_places[s] == (0 if s == 0 else 1))
        return lax.select_n(other, buf[k, part(s), :], buf[k, part(1 if s == 0 else 0), :])

    def chosen(k):
        parts = []
        for s in range(steps):
            parts.append(
                lax.select_n(
                    owners[s] <= z,
                    pick(above, k, n - 1 - z, dns, s),
                    pick(below, k, z, ups, s),
                )
            )
        return jnp.concatenate(parts, axis=0)

    def iteration(i, carry):
        hop(below, i, z, ups, lax.rem(z + 1, n), below_sem, up_send)
        hop(above, i, n - 1 - z, dns, lax.rem(z + n - 1, n), above_sem, dn_send)

        @pl.when((lax.rem(i, group) == 0) & (i < nw))
        def _():
            p = i // group
            total = jnp.zeros((slots, pw), F32)
            for s in range(steps):
                total = total + jnp.dot(
                    pack[s], states_ref[s, :, piece_lanes(p)], preferred_element_type=F32
                )
            xout[p] = total.astype(BF16)
            exchange(xout, arrived, p, pl.ds(0, pw), x_send, x_sem)

        k = i - SKEW * (n - 1)

        @pl.when((k >= 0) & (k < nw) & (lax.rem(k, group) == 0))
        def _():
            wait_exchange(arrived, k // group, x_sem)

        @pl.when((k >= 0) & (k < nw))
        def _():
            low_acc[...] += lax.dot_general(
                arrived[k // group, :, lanes(lax.rem(k, group))],
                chosen(k),
                (((1,), (1,)), ((), ())),
                preferred_element_type=F32,
            )

        @pl.when(k == nw - 1)
        def _():
            of_row = lax.rem(lax.broadcasted_iota(jnp.int32, low.shape, 0), block) // cap
            of_col = lax.broadcasted_iota(jnp.int32, low.shape, 1) // rank
            low[...] = jnp.where(of_row == of_col, low_acc[...], 0.0).astype(BF16)

        @pl.when((k >= nw) & (k < nch))
        def _():
            w = k - nw
            dout[w // group, :, lanes(lax.rem(w, group))] = jnp.dot(
                low[...], chosen(k), preferred_element_type=F32
            ).astype(BF16)

        @pl.when((k >= nw) & (k < nch - group) & (lax.rem(k - nw, group) == group - 1))
        def _():
            exchange(dout, returned, (k - nw) // group, pl.ds(0, pw), d_send, d_sem)

        @pl.when((k >= nch - group) & (k < nch))
        def _():
            span = lanes(lax.rem(k - nw, group))
            exchange(dout, returned, pieces - 1, span, d_send, d_sem)

        w_out = k - nw - LAG

        @pl.when((w_out >= 0) & (w_out < nw) & (lax.rem(w_out, group) == group - 1))
        def _():
            p = w_out // group
            wait_exchange(returned, p, d_sem)
            for s in range(steps):
                out_ref[s, :, piece_lanes(p)] = jnp.dot(
                    unpack[s], returned[p], preferred_element_type=F32
                ).astype(BF16)

        return carry

    lax.fori_loop(0, nch + SKEW * (n - 1) + LAG, iteration, 0)

    wait_sent(below, z, up_send)
    wait_sent(above, n - 1 - z, dn_send)
    for buf, sem in ((xout, x_send), (dout, d_send)):
        sent = buf.at[:, pl.ds(0, slots - block)]
        pltpu.make_async_copy(sent, sent, sem).wait()


def body(n, cols, states, request_slot_index, down_weights, up_weights, active_adapter_owner):
    steps, rows, width = states.shape
    rank = down_weights.shape[1]
    cap = max(2, 2 * rows // cols)
    block = -(-steps * cap // 16) * 16
    slots = cols * block
    wc = min(WIDTH, width)
    nw = width // wc
    group = GROUP if nw % GROUP == 0 else 1
    vmem = pl.BlockSpec(memory_space=pltpu.VMEM)
    hbm = pl.BlockSpec(memory_space=pl.ANY)
    dma = pltpu.SemaphoreType.DMA
    stream = pltpu.VMEM((2 * nw, steps * rank, wc), BF16)
    piece = pltpu.VMEM((nw // group, slots, wc * group), BF16)
    return pl.pallas_call(
        functools.partial(kernel, n, cols, steps, cap, block, wc, group),
        out_shape=pltpu.VMEM(states.shape, states.dtype),
        in_specs=[pl.BlockSpec(memory_space=pltpu.SMEM), vmem, hbm, hbm, hbm],
        out_specs=vmem,
        scratch_shapes=[
            pltpu.VMEM(states.shape, BF16),
            pltpu.VMEM(down_weights.shape, BF16),
            pltpu.VMEM(up_weights.shape, BF16),
            stream, stream, piece, piece, piece, piece,
            pltpu.VMEM((slots, steps * rank), F32),
            pltpu.VMEM((slots, steps * rank), BF16),
            pltpu.VMEM((steps, slots, rows), BF16),
            pltpu.VMEM((steps, rows, slots), BF16),
            dma((3,)), dma, dma, dma, dma,
            dma((2 * nw,)), dma((2 * nw,)), dma((nw // group,)), dma((nw // group,)),
        ],
        compiler_params=pltpu.CompilerParams(
            collective_id=0, has_side_effects=True, vmem_limit_bytes=56 * 1024 * 1024
        ),
    )(active_adapter_owner, request_slot_index[:, :, 0], states, down_weights, up_weights)


TOKEN_CHUNKS = 14
EARLY = 4
PAIR = 2
TO_MID, FROM_MID, FROM_IN = 2, 5, 8
OUT_LAG = 5
DONE_IN, DONE_OUT = 3, 3


def split_kernel(
    cols, steps, cap, wc, nt, early,
    owner_ref, slot_ref, states_any, down_any, up_any, out_ref,
    states_ref, dt, wcat, raw, u_out, v_out, u_in, v_in, m_out, inb, fin,
    xt_out, xt_in, xw_out, xw_in, dout, returned,
    acc, low_acc, low, lm_out, lm_in, lo_in, pack_t, pack_w, unpack,
    in_sem, raw_send, u_send, v_send, m_send, f_send, xt_send, xw_send, d_send, lm_send,
    raw_sem, u_sem, v_sem, in_pos, xt_sem, xw_sem, d_sem, lm_sem, lo_sem,
):
    z = lax.axis_index("dp")
    me = lax.axis_index("adapter")
    rows, width = states_any.shape[1:]
    rank = down_any.shape[1]
    block = steps * cap
    slots = cols * block
    half = wc // 2
    nc = width // wc
    nw = nc - nt
    npos = nw + nc
    pw = PAIR * wc
    nd = nc // PAIR
    low_tick = early + 2 * nt + FROM_MID - 1
    roles = [(low_tick + DONE_IN, nw + FROM_MID), (low_tick + DONE_OUT, nw + FROM_IN)]
    bulks = [min(max(done - base, 0), nd) for done, base in roles]
    ends = [
        max(done + bulk, base + 2 * nd) if bulk < nd else done + bulk
        for (done, base), bulk in zip(roles, bulks)
    ]
    plow_tick = early + FROM_IN + nt // 2
    xw_tick = nt // PAIR

    far = z // 2
    is_outer = (z == 0) | (z == 3)
    is_inner = (z == 1) | (z == 2)
    inner_z = 1 + far
    outer_z = 3 * far
    mid_z = 2 - far
    across_z = jnp.where(is_inner, 3 - outer_z, 3 - inner_z)
    done_tick = jnp.where(is_inner, roles[0][0], roles[1][0])
    base_tick = jnp.where(is_inner, roles[0][1], roles[1][1])
    bulk = jnp.where(is_inner, bulks[0], bulks[1])

    owners = [owner_ref[s, me] for s in range(steps)]
    by_in = [a == inner_z for a in owners]
    by_out = [a == outer_z for a in owners]
    mine = [i | o for i, o in zip(by_in, by_out)]
    any_out = by_out[0] | by_out[1]

    def lanes(k, n):
        return pl.ds(pl.multiple_of(k * n, n), n)

    def block_rows(j):
        return pl.ds(pl.multiple_of(j * block, block), block)

    tw = nt * wc
    loads = [
        pltpu.make_async_copy(src, dst, in_sem.at[i])
        for i, (src, dst) in enumerate(
            (
                (states_any, states_ref),
                (up_any.at[0], wcat.at[:, pl.ds(nw * wc, width)]),
                (down_any.at[0, :, pl.ds(tw, nw * wc)], wcat.at[:, pl.ds(0, nw * wc)]),
                (down_any.at[0, :, pl.ds(0, tw)], dt),
            )
        )
    ]
    for load in loads:
        load.start()

    barrier = pltpu.get_barrier_semaphore()
    for o in range(1, cols):
        pl.semaphore_signal(
            barrier, inc=1, device_id={"adapter": lax.rem(me + o, cols)}, device_id_type=MESH
        )

    pl.semaphore_signal(barrier, inc=1, device_id={"dp": across_z}, device_id_type=MESH)

    @pl.when(z > 0)
    def _():
        pl.semaphore_signal(barrier, inc=1, device_id={"dp": z - 1}, device_id_type=MESH)

    @pl.when(z < 3)
    def _():
        pl.semaphore_signal(barrier, inc=1, device_id={"dp": z + 1}, device_id_type=MESH)

    r_sub = lax.broadcasted_iota(jnp.int32, (rows, rows), 0)
    r_lane = lax.broadcasted_iota(jnp.int32, (rows, rows), 1)
    for s in range(steps):
        crow = slot_ref[s : s + 1, :]
        crow_b = jnp.broadcast_to(crow, (rows, rows))
        ccol = jnp.sum(jnp.where(r_sub == r_lane, crow_b, 0), axis=1, keepdims=True)
        same = jnp.broadcast_to(ccol, (rows, rows)) == crow_b
        rank_row = jnp.sum(jnp.where(same & (r_sub < r_lane), 1, 0), axis=0, keepdims=True)
        rank_col = jnp.sum(jnp.where(same & (r_lane < r_sub), 1, 0), axis=1, keepdims=True)
        at = lax.broadcasted_iota(jnp.int32, (slots, rows), 0)
        for g in range(2):
            pack_t[s, g] = jnp.where(at == crow * block + g * cap + rank_row, 1.0, 0.0).astype(BF16)
        pack_w[s] = jnp.where(at == crow * block + s * cap + rank_row, 1.0, 0.0).astype(BF16)
        unpack[s] = jnp.where(
            lax.broadcasted_iota(jnp.int32, (rows, slots), 1) == ccol * block + s * cap + rank_col,
            1.0,
            0.0,
        ).astype(BF16)
    low_acc[...] = jnp.zeros_like(low_acc)
    acc[...] = jnp.zeros_like(acc)

    for load in loads:
        load.wait()
    pl.semaphore_wait(barrier, cols + (z > 0).astype(jnp.int32) + (z < 3).astype(jnp.int32))

    partners = []
    for o in range(cols - 1, 0, -1):
        peer, bit = 0, 1
        while bit < cols:
            peer = peer + bit * lax.rem(lax.rem(me // bit, 2) + o // bit % 2, 2)
            bit = 2 * bit
        partners.append(peer if bit == cols else lax.rem(me + o, cols))

    def exchange(src, dst, w, span, send_sem, recv_sem):
        for peer in partners:
            pltpu.make_async_remote_copy(
                src_ref=src.at[w, block_rows(peer), span],
                dst_ref=dst.at[w, block_rows(me), span],
                send_sem=send_sem,
                recv_sem=recv_sem.at[w],
                device_id={"adapter": peer},
                device_id_type=MESH,
            ).start()
        dst[w, block_rows(me), span] = src[w, block_rows(me), span]

    def wait_exchange(dst, w, recv_sem):
        remote = dst.at[w, pl.ds(0, slots - block)]
        pltpu.make_async_copy(remote, remote, recv_sem.at[w]).wait()

    def along(src, dst, target, send_sem, recv_sem):
        return pltpu.make_async_remote_copy(
            src_ref=src,
            dst_ref=dst,
            send_sem=send_sem,
            recv_sem=recv_sem,
            device_id={"dp": target},
            device_id_type=MESH,
        )

    def folded(x):
        return jnp.concatenate([x[:, :half], x[:, half:]], axis=0)

    def unfolded(x):
        return jnp.concatenate([x[:rank], x[rank:]], axis=1)

    def across(a, b):
        return lax.dot_general(a, b, (((1,), (1,)), ((), ())), preferred_element_type=F32)

    def token(t, s):
        return xt_in[t // PAIR, :, lanes(s * PAIR + lax.rem(t, PAIR), half)]

    def chunk_at(p):
        return lax.rem(p + npos - early, npos)

    def both(p):
        return jnp.concatenate([unfolded(fin[p, s]) for s in range(steps)], axis=0)

    def known(w):
        own = folded(wcat[:, lanes(w, wc)])
        theirs = folded(raw[:, lanes(w, wc)])
        return [lax.select_n(by_in[s], theirs, own) for s in range(steps)]

    def iteration(i, carry):
        @pl.when(is_outer & (i < npos))
        def _():
            w = chunk_at(i)
            along(
                wcat.at[:, lanes(w, wc)], raw.at[:, lanes(w, wc)], inner_z, raw_send, raw_sem.at[w]
            ).start()

        @pl.when(i < nt // PAIR)
        def _():
            for s in range(steps):
                packs = jnp.concatenate([pack_t[s, g] for g in range(2)], axis=1)
                parts = []
                for c in range(PAIR):
                    wide = states_ref[s, :, lanes(i * PAIR + c, wc)]
                    parts.append(jnp.concatenate([wide[:, :half], wide[:, half:]], axis=0))
                xt_out[i, :, pl.ds(s * PAIR * half, PAIR * half)] = jnp.dot(
                    packs, jnp.concatenate(parts, axis=1), preferred_element_type=F32
                ).astype(BF16)
            exchange(xt_out, xt_in, i, pl.ds(0, pw), xt_send, xt_sem)

        a = i - xw_tick

        @pl.when((a >= 0) & (a < nw // PAIR))
        def _():
            packs = jnp.concatenate([pack_w[s] for s in range(steps)], axis=1)
            wide = jnp.concatenate(
                [states_ref[s, :, lanes(nt // PAIR + a, pw)] for s in range(steps)], axis=0
            )
            xw_out[a] = jnp.dot(packs, wide, preferred_element_type=F32).astype(BF16)
            exchange(xw_out, xw_in, a, pl.ds(0, pw), xw_send, xw_sem)

        @pl.when(is_outer & (i < npos))
        def _():
            t = i - early

            @pl.when((t >= 0) & (t < nt))
            def _():
                @pl.when(lax.rem(t, PAIR) == 0)
                def _():
                    wait_exchange(xt_in, t // PAIR, xt_sem)

                mine_t = folded(dt[:, lanes(t, wc)])
                u_out[t] = lax.select_n(any_out, token(t, 0), mine_t)
                along(u_out.at[t], u_in.at[t], inner_z, u_send, u_sem.at[t]).start()
                v_out[t] = lax.select_n(by_out[1], token(t, 1), token(t, 0))
                for s in range(steps):
                    acc[0, s, 0:slots] += across(token(t, s), mine_t)

            @pl.when((t >= nt) & (t < 2 * nt))
            def _():
                along(v_out.at[t - nt], v_in.at[t - nt], inner_z, v_send, v_sem.at[t - nt]).start()

        p = i - TO_MID

        @pl.when(is_inner & (p >= 0) & (p < npos))
        def _():
            w = chunk_at(p)
            theirs = raw.at[:, lanes(w, wc)]
            along(theirs, theirs, inner_z, raw_send, raw_sem.at[w]).wait_recv()
            weights = known(w)
            t = p - early

            @pl.when((t < 0) | (t >= 2 * nt))
            def _():
                for s in range(steps):
                    m_out[p, s] = weights[s]

            @pl.when((t >= 0) & (t < nt))
            def _():
                @pl.when(lax.rem(t, PAIR) == 0)
                def _():
                    wait_exchange(xt_in, t // PAIR, xt_sem)

                for s in range(steps):
                    m_out[p, s] = lax.select_n(mine[s], token(t, s), weights[s])

            @pl.when((t >= nt) & (t < 2 * nt))
            def _():
                v = t - nt
                along(v_out.at[v], v_in.at[v], inner_z, v_send, v_sem.at[v]).wait_recv()
                first = lax.select_n(by_out[1], u_in[v], v_in[v])
                m_out[p, 0] = lax.select_n(mine[0], first, weights[0])
                m_out[p, 1] = lax.select_n(mine[1], v_in[v], weights[1])

            for s in range(steps):
                along(m_out.at[p, s], inb.at[p, s], mid_z, m_send, in_pos.at[p, s]).start()

        q = i - FROM_MID

        @pl.when(is_inner & (q >= 0) & (q < npos))
        def _():
            weights = known(chunk_at(q))
            for s in range(steps):
                here = inb.at[q, s]
                along(here, here, mid_z, m_send, in_pos.at[q, s]).wait_recv()
                fin[q, s] = lax.select_n(mine[s], inb[q, s], weights[s])
                along(fin.at[q, s], here, outer_z, f_send, in_pos.at[q, s]).start()
            t = q - early

            @pl.when((t >= 0) & (t < nt))
            def _():
                along(u_out.at[t], u_in.at[t], inner_z, u_send, u_sem.at[t]).wait_recv()
                mine_t = folded(dt[:, lanes(t, wc)])
                for s in range(steps):
                    table = lax.select_n(by_out[s], mine_t, u_in[t])
                    given = jnp.concatenate([token(t, s), inb[q, s]], axis=0)
                    acc[0, s] += across(given, table)

            @pl.when((t >= nt) & (t < 2 * nt))
            def _():
                v = t - nt
                mine_t = folded(dt[:, lanes(v, wc)])
                for s in range(steps):
                    table = lax.select_n(by_out[s], mine_t, u_in[v])
                    theirs = v_in[v]
                    if s == 0:
                        theirs = lax.select_n(by_out[1], u_in[v], theirs)
                    given = jnp.concatenate([theirs, inb[q, s]], axis=0)
                    acc[1, s] += across(given, table)

        r = i - FROM_IN

        @pl.when(is_outer & (r >= 0) & (r < npos))
        def _():
            own = folded(wcat[:, lanes(chunk_at(r), wc)])
            for s in range(steps):
                here = inb.at[r, s]
                along(here, here, outer_z, f_send, in_pos.at[r, s]).wait_recv()
                fin[r, s] = lax.select_n(by_out[s], inb[r, s], own)

        c = i - plow_tick

        @pl.when((c >= 0) & (c < nw))
        def _():
            @pl.when(lax.rem(c, PAIR) == 0)
            def _():
                wait_exchange(xw_in, c // PAIR, xw_sem)

            low_acc[...] += across(
                xw_in[c // PAIR, :, lanes(lax.rem(c, PAIR), wc)], both(early + c)
            )

        lane = lax.broadcasted_iota(jnp.int32, (cols * cap, steps * rank), 1)

        def per_step(flags):
            return jnp.where(lane < rank, flags[0].astype(jnp.int32), flags[1].astype(jnp.int32)) != 0

        def reduced(k, part):
            out = []
            for s in range(steps):
                x = acc[k, s, part * slots : (part + 1) * slots].reshape(cols, 2, cap, 2 * rank)
                x = [x[:, g].reshape(cols * cap, 2 * rank) for g in range(2)]
                x[1 - s] = pltpu.roll(x[1 - s], rank, axis=1)
                out.append(x[0] + x[1])
            return jnp.where(lane < rank, out[0], out[1])

        @pl.when(is_inner & (i == low_tick))
        def _():
            lm_out[0] = reduced(0, 1).astype(BF16)
            lm_out[1] = reduced(1, 1).astype(BF16)
            lm_out[2] = reduced(1, 0).astype(BF16)
            along(lm_out.at[0], lm_in, mid_z, lm_send, lm_sem).start()
            along(lm_out.at[1], lo_in.at[1], across_z, lm_send, lo_sem.at[1]).start()
            along(lm_out.at[2], lo_in.at[0], outer_z, lm_send, lo_sem.at[0]).start()

        def finish(part):
            spread = jnp.broadcast_to(
                part.reshape(cols, 1, cap, steps * rank), (cols, steps, cap, steps * rank)
            ).reshape(slots, steps * rank)
            of_row = lax.rem(lax.broadcasted_iota(jnp.int32, low.shape, 0), block) // cap
            of_col = lax.broadcasted_iota(jnp.int32, low.shape, 1) // rank
            low[...] = jnp.where(of_row == of_col, low_acc[...] + spread, 0.0).astype(BF16)

        @pl.when(is_inner & (i == done_tick))
        def _():
            along(lm_out.at[0], lm_in, mid_z, lm_send, lm_sem).wait_recv()
            finish(jnp.where(per_step(mine), reduced(0, 0), lm_in[...].astype(F32)))

        @pl.when(is_outer & (i == done_tick))
        def _():
            for k in range(2):
                along(lm_out.at[2 - k], lo_in.at[k], outer_z, lm_send, lo_sem.at[k]).wait_recv()
            theirs = jnp.where(per_step(by_in), lo_in[0].astype(F32), lo_in[1].astype(F32))
            finish(jnp.where(per_step(by_out), reduced(0, 0), theirs))

        def place(v):
            return lax.rem(v + nd - early // PAIR, nd)

        def deltas(v, c):
            u = v * PAIR + c
            at = u + jnp.where(u < early, 0, nw)
            dout[place(v), :, lanes(c, wc)] = jnp.dot(
                low[...], both(at), preferred_element_type=F32
            ).astype(BF16)

        v = i - done_tick

        @pl.when((v >= 0) & (v < bulk))
        def _():
            for c in range(PAIR):
                deltas(v, c)
            exchange(dout, returned, place(v), pl.ds(0, pw), d_send, d_sem)

        n = i - base_tick

        @pl.when((n >= bulk * PAIR) & (n < nd * PAIR))
        def _():
            deltas(n // PAIR, lax.rem(n, PAIR))
            span = lanes(lax.rem(n, PAIR), wc)
            exchange(dout, returned, place(n // PAIR), span, d_send, d_sem)

        def gather(e):
            wait_exchange(returned, e, d_sem)
            for s in range(steps):
                out_ref[s, :, lanes(e, pw)] = jnp.dot(
                    unpack[s], returned[e], preferred_element_type=F32
                ).astype(BF16)

        v_back = v - OUT_LAG

        @pl.when((v_back >= 0) & (v_back < bulk))
        def _():
            gather(place(v_back))

        n_back = n - OUT_LAG - 1

        @pl.when((n_back >= bulk * PAIR) & (n_back < nd * PAIR) & (lax.rem(n_back, PAIR) == 0))
        def _():
            gather(place(n_back // PAIR))

        return carry

    lax.fori_loop(0, max(ends) + OUT_LAG + 1, iteration, 0)

    @pl.when(is_outer)
    def _():
        for buf, sem in ((wcat, raw_send), (u_out, u_send), (v_out, v_send)):
            pltpu.make_async_copy(buf, buf, sem).wait()

    @pl.when(is_inner)
    def _():
        for buf, sem in ((m_out, m_send), (fin, f_send), (lm_out, lm_send)):
            pltpu.make_async_copy(buf, buf, sem).wait()

    for buf, sem in ((xt_out, xt_send), (xw_out, xw_send), (dout, d_send)):
        sent = buf.at[:, pl.ds(0, slots - block)]
        pltpu.make_async_copy(sent, sent, sem).wait()


def split_body(cols, states, request_slot_index, down_weights, up_weights, active_adapter_owner):
    steps, rows, width = states.shape
    rank = down_weights.shape[1]
    cap = 2 * rows // cols
    slots = cols * steps * cap
    wc = WIDTH
    nc = width // wc
    nt = TOKEN_CHUNKS * nc // 32
    nw = nc - nt
    npos = nw + nc
    early = EARLY
    vmem = pl.BlockSpec(memory_space=pltpu.VMEM)
    hbm = pl.BlockSpec(memory_space=pl.ANY)
    dma = pltpu.SemaphoreType.DMA
    fold = (2 * rank, wc // 2)
    tokens = pltpu.VMEM((nt // PAIR, slots, PAIR * wc), BF16)
    others = pltpu.VMEM((nw // PAIR, slots, PAIR * wc), BF16)
    deltas = pltpu.VMEM((nc // PAIR, slots, PAIR * wc), BF16)
    side = pltpu.VMEM((nt, *fold), BF16)
    stream = pltpu.VMEM((npos, steps, *fold), BF16)
    line = pltpu.VMEM((rank, npos * wc), BF16)
    lows = (cols * cap, steps * rank)
    return pl.pallas_call(
        functools.partial(split_kernel, cols, steps, cap, wc, nt, early),
        out_shape=pltpu.VMEM(states.shape, states.dtype),
        in_specs=[pl.BlockSpec(memory_space=pltpu.SMEM), vmem, hbm, hbm, hbm],
        out_specs=vmem,
        scratch_shapes=[
            pltpu.VMEM(states.shape, BF16),
            pltpu.VMEM((rank, nt * wc), BF16),
            line, line, side, side, side, side, stream, stream, stream,
            tokens, tokens, others, others, deltas, deltas,
            pltpu.VMEM((2, steps, 2 * slots, 2 * rank), F32),
            pltpu.VMEM((slots, steps * rank), F32),
            pltpu.VMEM((slots, steps * rank), BF16),
            pltpu.VMEM((3, *lows), BF16), pltpu.VMEM(lows, BF16), pltpu.VMEM((2, *lows), BF16),
            pltpu.VMEM((steps, 2, slots, rows), BF16),
            pltpu.VMEM((steps, slots, rows), BF16),
            pltpu.VMEM((steps, rows, slots), BF16),
            dma((4,)), dma, dma, dma, dma, dma, dma, dma, dma, dma,
            dma((npos,)), dma((nt,)), dma((nt,)), dma((npos, steps)),
            dma((nt // PAIR,)), dma((nw // PAIR,)), dma((nc // PAIR,)), dma, dma((2,)),
        ],
        compiler_params=pltpu.CompilerParams(
            collective_id=0, has_side_effects=True, vmem_limit_bytes=56 * 1024 * 1024
        ),
    )(active_adapter_owner, request_slot_index[:, :, 0], states, down_weights, up_weights)


def routed(n, cols, states, request_slot_index, down_weights, up_weights, active_adapter_owner):
    steps, rows, width = states.shape
    cap = 2 * rows // cols
    paired = steps == 2 and cap == 8 and cols * cap == down_weights.shape[1]
    if n == 4 and paired and width % (8 * WIDTH) == 0:
        run = functools.partial(split_body, cols)
    else:
        run = functools.partial(body, n, cols)
    return run(states, request_slot_index, down_weights, up_weights, active_adapter_owner)


def solution(mesh):
    return jax.shard_map(
        functools.partial(routed, mesh.shape["dp"], mesh.shape["adapter"]),
        mesh=mesh,
        in_specs=(
            P(None, ("dp", "adapter"), None),
            P(None, ("dp", "adapter"), None),
            P(("dp", "adapter"), None, None),
            P(("dp", "adapter"), None, None),
            P(),
        ),
        out_specs=P(None, ("dp", "adapter"), None),
        check_vma=False,
    )
```

```python
import functools

import jax
import jax.numpy as jnp
from jax import lax
from jax.experimental import pallas as pl
from jax.experimental.pallas import tpu as pltpu
from jax.sharding import PartitionSpec as P

MESH = pl.DeviceIdType.MESH
F32 = jnp.float32
BF16 = jnp.bfloat16
WIDTH = 256
SKEW = 3
LAG = 3
GROUP = 2


def kernel(
    n, cols, steps, cap, block, wc, group,
    owner_ref, slot_ref, states_any, down_any, up_any, out_ref,
    states_ref, down_ref, up_ref, below, above, xout, arrived, dout, returned, low_acc, low, pack, unpack,
    in_sem, up_send, dn_send, x_send, d_send, below_sem, above_sem, x_sem, d_sem,
):
    z = lax.axis_index("dp")
    me = lax.axis_index("adapter")
    rows = states_any.shape[1]
    rank = down_any.shape[1]
    nw = states_any.shape[2] // wc
    nch = 2 * nw
    slots = cols * block
    not_first = z > 0
    not_last = z < n - 1

    pieces = nw // group
    pw = wc * group
    loads = [
        pltpu.make_async_copy(src, dst, in_sem.at[i])
        for i, (src, dst) in enumerate(
            ((down_any, down_ref), (up_any, up_ref), (states_any, states_ref))
        )
    ]
    for load in loads:
        load.start()

    def lanes(w):
        return pl.ds(pl.multiple_of(w * wc, wc), wc)

    def piece_lanes(p):
        return pl.ds(pl.multiple_of(p * pw, pw), pw)

    def block_rows(j):
        return pl.ds(pl.multiple_of(j * block, block), block)

    barrier = pltpu.get_barrier_semaphore()
    for o in range(1, cols):
        pl.semaphore_signal(
            barrier, inc=1, device_id={"adapter": lax.rem(me + o, cols)}, device_id_type=MESH
        )

    @pl.when(not_first)
    def _():
        pl.semaphore_signal(barrier, inc=1, device_id={"dp": z - 1}, device_id_type=MESH)

    @pl.when(not_last)
    def _():
        pl.semaphore_signal(barrier, inc=1, device_id={"dp": z + 1}, device_id_type=MESH)

    r_sub = lax.broadcasted_iota(jnp.int32, (rows, rows), 0)
    r_lane = lax.broadcasted_iota(jnp.int32, (rows, rows), 1)
    for s in range(steps):
        crow = slot_ref[s : s + 1, :]
        crow_b = jnp.broadcast_to(crow, (rows, rows))
        ccol = jnp.sum(jnp.where(r_sub == r_lane, crow_b, 0), axis=1, keepdims=True)
        same = jnp.broadcast_to(ccol, (rows, rows)) == crow_b
        rank_row = jnp.sum(jnp.where(same & (r_sub < r_lane), 1, 0), axis=0, keepdims=True)
        rank_col = jnp.sum(jnp.where(same & (r_lane < r_sub), 1, 0), axis=1, keepdims=True)
        trow = crow * block + s * cap + rank_row
        tcol = ccol * block + s * cap + rank_col
        pack[s] = jnp.where(
            lax.broadcasted_iota(jnp.int32, (slots, rows), 0) == trow, 1.0, 0.0
        ).astype(BF16)
        unpack[s] = jnp.where(
            lax.broadcasted_iota(jnp.int32, (rows, slots), 1) == tcol, 1.0, 0.0
        ).astype(BF16)
    low_acc[...] = jnp.zeros_like(low_acc)

    owners = [owner_ref[s, me] for s in range(steps)]
    for load in loads:
        load.wait()
    pl.semaphore_wait(
        barrier, cols - 1 + not_first.astype(jnp.int32) + not_last.astype(jnp.int32)
    )

    def own(k, use):
        @pl.when(k < nw)
        def _():
            use(down_ref[0, :, lanes(k)])

        @pl.when(k >= nw)
        def _():
            use(up_ref[0, :, lanes(k - nw)])

    def part(s):
        return pl.ds(s * rank, rank)

    def hop(buf, i, place, owner_places, target, recv_sem, send_sem):
        def copy(k, src, dst):
            return pltpu.make_async_remote_copy(
                src_ref=buf.at[k, src],
                dst_ref=buf.at[k, dst],
                send_sem=send_sem,
                recv_sem=recv_sem.at[k],
                device_id={"dp": target},
                device_id_type=MESH,
            )

        whole = pl.ds(0, steps * rank)
        second = i - SKEW
        later = i - SKEW * place

        @pl.when((place == 0) & (i < nch))
        def _():
            def use(mine):
                for s in range(steps):
                    buf[i, part(s), :] = mine

            own(i, use)
            copy(i, part(0), part(1)).start()

        @pl.when((place == 1) & (i < nch))
        def _():
            def use(mine):
                buf[i, part(0), :] = mine

            own(i, use)

            @pl.when(place < n - 1)
            def _():
                copy(i, part(0), part(0)).start()

        @pl.when((place == 1) & (second >= 0) & (second < nch))
        def _():
            copy(second, part(1), part(1)).wait_recv()

            @pl.when(place < n - 1)
            def _():
                copy(second, part(1), part(1)).start()

        @pl.when((place > 1) & (later >= 0) & (later < nch))
        def _():
            copy(later, whole, whole).wait_recv()

            def use(mine):
                theirs = [buf[later, part(s), :] for s in range(steps)]
                for s in range(steps):
                    value = theirs[s]
                    raw = place == 2
                    if s == 0:
                        value = lax.select_n(raw & (owner_places[s] == 0), value, theirs[1])
                    else:
                        value = lax.select_n(raw & (owner_places[s] == 0), value, theirs[1])
                        value = lax.select_n(raw & (owner_places[s] == 1), value, theirs[0])
                    buf[later, part(s), :] = lax.select_n(owner_places[s] == place, value, mine)

            own(later, use)

            @pl.when(place < n - 1)
            def _():
                copy(later, whole, whole).start()

    def wait_sent(buf, place, send_sem):
        @pl.when(place == 0)
        def _():
            sent = buf.at[:, part(0)]
            pltpu.make_async_copy(sent, sent, send_sem).wait()

        @pl.when((place > 0) & (place < n - 1))
        def _():
            pltpu.make_async_copy(buf, buf, send_sem).wait()

    partners = []
    for o in range(cols - 1, 0, -1):
        peer, bit = 0, 1
        while bit < cols:
            peer = peer + bit * lax.rem(lax.rem(me // bit, 2) + o // bit % 2, 2)
            bit = 2 * bit
        partners.append(peer if bit == cols else lax.rem(me + o, cols))

    def exchange(src, dst, w, span, send_sem, recv_sem):
        for peer in partners:
            pltpu.make_async_remote_copy(
                src_ref=src.at[w, block_rows(peer), span],
                dst_ref=dst.at[w, block_rows(me), span],
                send_sem=send_sem,
                recv_sem=recv_sem.at[w],
                device_id={"adapter": peer},
                device_id_type=MESH,
            ).start()
        dst[w, block_rows(me), span] = src[w, block_rows(me), span]

    def wait_exchange(dst, w, recv_sem):
        remote = dst.at[w, pl.ds(0, slots - block)]
        pltpu.make_async_copy(remote, remote, recv_sem.at[w]).wait()

    ups = owners
    dns = [n - 1 - owner for owner in owners]

    def pick(buf, k, place, owner_places, s):
        other = (place == 1) & (owner_places[s] == (0 if s == 0 else 1))
        return lax.select_n(other, buf[k, part(s), :], buf[k, part(1 if s == 0 else 0), :])

    def chosen(k):
        parts = []
        for s in range(steps):
            parts.append(
                lax.select_n(
                    owners[s] <= z,
                    pick(above, k, n - 1 - z, dns, s),
                    pick(below, k, z, ups, s),
                )
            )
        return jnp.concatenate(parts, axis=0)

    def iteration(i, carry):
        hop(below, i, z, ups, lax.rem(z + 1, n), below_sem, up_send)
        hop(above, i, n - 1 - z, dns, lax.rem(z + n - 1, n), above_sem, dn_send)

        @pl.when((lax.rem(i, group) == 0) & (i < nw))
        def _():
            p = i // group
            total = jnp.zeros((slots, pw), F32)
            for s in range(steps):
                total = total + jnp.dot(
                    pack[s], states_ref[s, :, piece_lanes(p)], preferred_element_type=F32
                )
            xout[p] = total.astype(BF16)
            exchange(xout, arrived, p, pl.ds(0, pw), x_send, x_sem)

        k = i - SKEW * (n - 1)

        @pl.when((k >= 0) & (k < nw) & (lax.rem(k, group) == 0))
        def _():
            wait_exchange(arrived, k // group, x_sem)

        @pl.when((k >= 0) & (k < nw))
        def _():
            low_acc[...] += lax.dot_general(
                arrived[k // group, :, lanes(lax.rem(k, group))],
                chosen(k),
                (((1,), (1,)), ((), ())),
                preferred_element_type=F32,
            )

        @pl.when(k == nw - 1)
        def _():
            of_row = lax.rem(lax.broadcasted_iota(jnp.int32, low.shape, 0), block) // cap
            of_col = lax.broadcasted_iota(jnp.int32, low.shape, 1) // rank
            low[...] = jnp.where(of_row == of_col, low_acc[...], 0.0).astype(BF16)

        @pl.when((k >= nw) & (k < nch))
        def _():
            w = k - nw
            dout[w // group, :, lanes(lax.rem(w, group))] = jnp.dot(
                low[...], chosen(k), preferred_element_type=F32
            ).astype(BF16)

        @pl.when((k >= nw) & (k < nch - group) & (lax.rem(k - nw, group) == group - 1))
        def _():
            exchange(dout, returned, (k - nw) // group, pl.ds(0, pw), d_send, d_sem)

        @pl.when((k >= nch - group) & (k < nch))
        def _():
            span = lanes(lax.rem(k - nw, group))
            exchange(dout, returned, pieces - 1, span, d_send, d_sem)

        w_out = k - nw - LAG

        @pl.when((w_out >= 0) & (w_out < nw) & (lax.rem(w_out, group) == group - 1))
        def _():
            p = w_out // group
            wait_exchange(returned, p, d_sem)
            for s in range(steps):
                out_ref[s, :, piece_lanes(p)] = jnp.dot(
                    unpack[s], returned[p], preferred_element_type=F32
                ).astype(BF16)

        return carry

    lax.fori_loop(0, nch + SKEW * (n - 1) + LAG, iteration, 0)

    wait_sent(below, z, up_send)
    wait_sent(above, n - 1 - z, dn_send)
    for buf, sem in ((xout, x_send), (dout, d_send)):
        sent = buf.at[:, pl.ds(0, slots - block)]
        pltpu.make_async_copy(sent, sent, sem).wait()


def body(n, cols, states, request_slot_index, down_weights, up_weights, active_adapter_owner):
    steps, rows, width = states.shape
    rank = down_weights.shape[1]
    cap = max(2, 2 * rows // cols)
    block = -(-steps * cap // 16) * 16
    slots = cols * block
    wc = min(WIDTH, width)
    nw = width // wc
    group = GROUP if nw % GROUP == 0 else 1
    vmem = pl.BlockSpec(memory_space=pltpu.VMEM)
    hbm = pl.BlockSpec(memory_space=pl.ANY)
    dma = pltpu.SemaphoreType.DMA
    stream = pltpu.VMEM((2 * nw, steps * rank, wc), BF16)
    piece = pltpu.VMEM((nw // group, slots, wc * group), BF16)
    return pl.pallas_call(
        functools.partial(kernel, n, cols, steps, cap, block, wc, group),
        out_shape=pltpu.VMEM(states.shape, states.dtype),
        in_specs=[pl.BlockSpec(memory_space=pltpu.SMEM), vmem, hbm, hbm, hbm],
        out_specs=vmem,
        scratch_shapes=[
            pltpu.VMEM(states.shape, BF16),
            pltpu.VMEM(down_weights.shape, BF16),
            pltpu.VMEM(up_weights.shape, BF16),
            stream, stream, piece, piece, piece, piece,
            pltpu.VMEM((slots, steps * rank), F32),
            pltpu.VMEM((slots, steps * rank), BF16),
            pltpu.VMEM((steps, slots, rows), BF16),
            pltpu.VMEM((steps, rows, slots), BF16),
            dma((3,)), dma, dma, dma, dma,
            dma((2 * nw,)), dma((2 * nw,)), dma((nw // group,)), dma((nw // group,)),
        ],
        compiler_params=pltpu.CompilerParams(
            collective_id=0, has_side_effects=True, vmem_limit_bytes=56 * 1024 * 1024
        ),
    )(active_adapter_owner, request_slot_index[:, :, 0], states, down_weights, up_weights)


TOKEN_CHUNKS = 14
EARLY = 4
PAIR = 2
TO_MID, FROM_MID, FROM_IN = 2, 5, 8
OUT_LAG = 5
DONE_IN, DONE_OUT = 3, 3


def split_kernel(
    cols, steps, cap, wc, nt, early,
    owner_ref, slot_ref, states_any, down_any, up_any, out_ref,
    states_ref, dt, wcat, raw, u_out, v_out, u_in, v_in, m_out, inb, fin,
    xt_out, xt_in, xw_out, xw_in, dout, returned,
    acc, low_acc, low, low_x, d_out, lm_out, lm_in, lo_in, pack_t, pack_w, unpack,
    in_sem, raw_send, u_send, v_send, m_send, f_send, xt_send, xw_send, d_send, lm_send, lx_send, dx_send,
    raw_sem, u_sem, v_sem, in_pos, xt_sem, xw_sem, d_sem, lm_sem, lo_sem, lx_sem,
):
    z = lax.axis_index("dp")
    me = lax.axis_index("adapter")
    rows, width = states_any.shape[1:]
    rank = down_any.shape[1]
    block = steps * cap
    slots = cols * block
    half = wc // 2
    nc = width // wc
    nw = nc - nt
    npos = nw + nc
    pw = PAIR * wc
    nd = nc // PAIR
    low_tick = early + 2 * nt + FROM_MID - 1
    roles = [(low_tick + DONE_IN, nw + FROM_MID), (low_tick + DONE_OUT, nw + FROM_IN)]
    counts = [nd, nd - 1]
    bulks = [min(max(done - base, 0), n) for (done, base), n in zip(roles, counts)]
    ends = [
        max(done + bulk, base + 2 * n) if bulk < n else done + bulk
        for (done, base), bulk, n in zip(roles, bulks, counts)
    ]
    last_tick = max(ends) + OUT_LAG
    last_place = nd - 1 - early // PAIR
    kept = npos - PAIR
    far_tick = max(kept + FROM_MID, roles[1][0] + 1)
    plow_tick = early + FROM_IN + nt // 2
    xw_tick = nt // PAIR

    far = z // 2
    is_outer = (z == 0) | (z == 3)
    is_inner = (z == 1) | (z == 2)
    inner_z = 1 + far
    outer_z = 3 * far
    mid_z = 2 - far
    across_z = jnp.where(is_inner, 3 - outer_z, 3 - inner_z)
    done_tick = jnp.where(is_inner, roles[0][0], roles[1][0])
    base_tick = jnp.where(is_inner, roles[0][1], roles[1][1])
    bulk = jnp.where(is_inner, bulks[0], bulks[1])
    count = jnp.where(is_inner, counts[0], counts[1])

    owners = [owner_ref[s, me] for s in range(steps)]
    by_in = [a == inner_z for a in owners]
    by_out = [a == outer_z for a in owners]
    mine = [i | o for i, o in zip(by_in, by_out)]
    any_out = by_out[0] | by_out[1]

    def lanes(k, n):
        return pl.ds(pl.multiple_of(k * n, n), n)

    def block_rows(j):
        return pl.ds(pl.multiple_of(j * block, block), block)

    tw = nt * wc
    loads = [
        pltpu.make_async_copy(src, dst, in_sem.at[i])
        for i, (src, dst) in enumerate(
            (
                (states_any, states_ref),
                (up_any.at[0], wcat.at[:, pl.ds(nw * wc, width)]),
                (down_any.at[0, :, pl.ds(tw, nw * wc)], wcat.at[:, pl.ds(0, nw * wc)]),
                (down_any.at[0, :, pl.ds(0, tw)], dt),
            )
        )
    ]
    for load in loads:
        load.start()

    barrier = pltpu.get_barrier_semaphore()
    for o in range(1, cols):
        pl.semaphore_signal(
            barrier, inc=1, device_id={"adapter": lax.rem(me + o, cols)}, device_id_type=MESH
        )

    pl.semaphore_signal(barrier, inc=1, device_id={"dp": across_z}, device_id_type=MESH)

    @pl.when(is_outer)
    def _():
        for o in range(1, cols):
            pl.semaphore_signal(
                barrier,
                inc=1,
                device_id={"dp": inner_z, "adapter": lax.rem(me + o, cols)},
                device_id_type=MESH,
            )

    @pl.when(z > 0)
    def _():
        pl.semaphore_signal(barrier, inc=1, device_id={"dp": z - 1}, device_id_type=MESH)

    @pl.when(z < 3)
    def _():
        pl.semaphore_signal(barrier, inc=1, device_id={"dp": z + 1}, device_id_type=MESH)

    r_sub = lax.broadcasted_iota(jnp.int32, (rows, rows), 0)
    r_lane = lax.broadcasted_iota(jnp.int32, (rows, rows), 1)
    for s in range(steps):
        crow = slot_ref[s : s + 1, :]
        crow_b = jnp.broadcast_to(crow, (rows, rows))
        ccol = jnp.sum(jnp.where(r_sub == r_lane, crow_b, 0), axis=1, keepdims=True)
        same = jnp.broadcast_to(ccol, (rows, rows)) == crow_b
        rank_row = jnp.sum(jnp.where(same & (r_sub < r_lane), 1, 0), axis=0, keepdims=True)
        rank_col = jnp.sum(jnp.where(same & (r_lane < r_sub), 1, 0), axis=1, keepdims=True)
        at = lax.broadcasted_iota(jnp.int32, (slots, rows), 0)
        for g in range(2):
            pack_t[s, g] = jnp.where(at == crow * block + g * cap + rank_row, 1.0, 0.0).astype(BF16)
        pack_w[s] = jnp.where(at == crow * block + s * cap + rank_row, 1.0, 0.0).astype(BF16)
        unpack[s] = jnp.where(
            lax.broadcasted_iota(jnp.int32, (rows, slots), 1) == ccol * block + s * cap + rank_col,
            1.0,
            0.0,
        ).astype(BF16)
    low_acc[...] = jnp.zeros_like(low_acc)
    acc[...] = jnp.zeros_like(acc)

    for load in loads:
        load.wait()
    pl.semaphore_wait(barrier, cols + jnp.where(is_inner, cols + 1, 1))

    partners = []
    for o in range(cols - 1, 0, -1):
        peer, bit = 0, 1
        while bit < cols:
            peer = peer + bit * lax.rem(lax.rem(me // bit, 2) + o // bit % 2, 2)
            bit = 2 * bit
        partners.append(peer if bit == cols else lax.rem(me + o, cols))

    def exchange(src, dst, w, span, send_sem, recv_sem):
        for peer in partners:
            pltpu.make_async_remote_copy(
                src_ref=src.at[w, block_rows(peer), span],
                dst_ref=dst.at[w, block_rows(me), span],
                send_sem=send_sem,
                recv_sem=recv_sem.at[w],
                device_id={"adapter": peer},
                device_id_type=MESH,
            ).start()
        dst[w, block_rows(me), span] = src[w, block_rows(me), span]

    def wait_exchange(dst, w, recv_sem):
        remote = dst.at[w, pl.ds(0, slots - block)]
        pltpu.make_async_copy(remote, remote, recv_sem.at[w]).wait()

    def along(src, dst, target, send_sem, recv_sem):
        return pltpu.make_async_remote_copy(
            src_ref=src,
            dst_ref=dst,
            send_sem=send_sem,
            recv_sem=recv_sem,
            device_id={"dp": target},
            device_id_type=MESH,
        )

    def folded(x):
        return jnp.concatenate([x[:, :half], x[:, half:]], axis=0)

    def unfolded(x):
        return jnp.concatenate([x[:rank], x[rank:]], axis=1)

    def across(a, b):
        return lax.dot_general(a, b, (((1,), (1,)), ((), ())), preferred_element_type=F32)

    def token(t, s):
        return xt_in[t // PAIR, :, lanes(s * PAIR + lax.rem(t, PAIR), half)]

    def chunk_at(p):
        return lax.rem(p + npos - early, npos)

    def both(p):
        return jnp.concatenate([unfolded(fin[p, s]) for s in range(steps)], axis=0)

    def known(w):
        own = folded(wcat[:, lanes(w, wc)])
        theirs = folded(raw[:, lanes(w, wc)])
        return [lax.select_n(by_in[s], theirs, own) for s in range(steps)]

    def iteration(i, carry):
        @pl.when(is_outer & (i < npos))
        def _():
            w = chunk_at(i)
            along(
                wcat.at[:, lanes(w, wc)], raw.at[:, lanes(w, wc)], inner_z, raw_send, raw_sem.at[w]
            ).start()

        @pl.when(i < nt // PAIR)
        def _():
            for s in range(steps):
                packs = jnp.concatenate([pack_t[s, g] for g in range(2)], axis=1)
                parts = []
                for c in range(PAIR):
                    wide = states_ref[s, :, lanes(i * PAIR + c, wc)]
                    parts.append(jnp.concatenate([wide[:, :half], wide[:, half:]], axis=0))
                xt_out[i, :, pl.ds(s * PAIR * half, PAIR * half)] = jnp.dot(
                    packs, jnp.concatenate(parts, axis=1), preferred_element_type=F32
                ).astype(BF16)
            exchange(xt_out, xt_in, i, pl.ds(0, pw), xt_send, xt_sem)

        a = i - xw_tick

        @pl.when((a >= 0) & (a < nw // PAIR))
        def _():
            packs = jnp.concatenate([pack_w[s] for s in range(steps)], axis=1)
            wide = jnp.concatenate(
                [states_ref[s, :, lanes(nt // PAIR + a, pw)] for s in range(steps)], axis=0
            )
            xw_out[a] = jnp.dot(packs, wide, preferred_element_type=F32).astype(BF16)
            exchange(xw_out, xw_in, a, pl.ds(0, pw), xw_send, xw_sem)

        @pl.when(is_outer & (i < npos))
        def _():
            t = i - early

            @pl.when((t >= 0) & (t < nt))
            def _():
                @pl.when(lax.rem(t, PAIR) == 0)
                def _():
                    wait_exchange(xt_in, t // PAIR, xt_sem)

                mine_t = folded(dt[:, lanes(t, wc)])
                u_out[t] = lax.select_n(any_out, token(t, 0), mine_t)
                along(u_out.at[t], u_in.at[t], inner_z, u_send, u_sem.at[t]).start()
                v_out[t] = lax.select_n(by_out[1], token(t, 1), token(t, 0))
                for s in range(steps):
                    acc[0, s, 0:slots] += across(token(t, s), mine_t)

            @pl.when((t >= nt) & (t < 2 * nt))
            def _():
                along(v_out.at[t - nt], v_in.at[t - nt], inner_z, v_send, v_sem.at[t - nt]).start()

        p = i - TO_MID

        @pl.when(is_inner & (p >= 0) & (p < npos))
        def _():
            w = chunk_at(p)
            theirs = raw.at[:, lanes(w, wc)]
            along(theirs, theirs, inner_z, raw_send, raw_sem.at[w]).wait_recv()
            weights = known(w)
            t = p - early

            @pl.when((t < 0) | (t >= 2 * nt))
            def _():
                for s in range(steps):
                    m_out[p, s] = weights[s]

            @pl.when((t >= 0) & (t < nt))
            def _():
                @pl.when(lax.rem(t, PAIR) == 0)
                def _():
                    wait_exchange(xt_in, t // PAIR, xt_sem)

                for s in range(steps):
                    m_out[p, s] = lax.select_n(mine[s], token(t, s), weights[s])

            @pl.when((t >= nt) & (t < 2 * nt))
            def _():
                v = t - nt
                along(v_out.at[v], v_in.at[v], inner_z, v_send, v_sem.at[v]).wait_recv()
                first = lax.select_n(by_out[1], u_in[v], v_in[v])
                m_out[p, 0] = lax.select_n(mine[0], first, weights[0])
                m_out[p, 1] = lax.select_n(mine[1], v_in[v], weights[1])

            for s in range(steps):
                along(m_out.at[p, s], inb.at[p, s], mid_z, m_send, in_pos.at[p, s]).start()

        q = i - FROM_MID

        @pl.when(is_inner & (q >= 0) & (q < npos))
        def _():
            weights = known(chunk_at(q))
            for s in range(steps):
                here = inb.at[q, s]
                along(here, here, mid_z, m_send, in_pos.at[q, s]).wait_recv()
                fin[q, s] = lax.select_n(mine[s], inb[q, s], weights[s])

                @pl.when(q < kept)
                def _():
                    along(fin.at[q, s], here, outer_z, f_send, in_pos.at[q, s]).start()

            t = q - early

            @pl.when((t >= 0) & (t < nt))
            def _():
                along(u_out.at[t], u_in.at[t], inner_z, u_send, u_sem.at[t]).wait_recv()
                mine_t = folded(dt[:, lanes(t, wc)])
                for s in range(steps):
                    table = lax.select_n(by_out[s], mine_t, u_in[t])
                    given = jnp.concatenate([token(t, s), inb[q, s]], axis=0)
                    acc[0, s] += across(given, table)

            @pl.when((t >= nt) & (t < 2 * nt))
            def _():
                v = t - nt
                mine_t = folded(dt[:, lanes(v, wc)])
                for s in range(steps):
                    table = lax.select_n(by_out[s], mine_t, u_in[v])
                    theirs = v_in[v]
                    if s == 0:
                        theirs = lax.select_n(by_out[1], u_in[v], theirs)
                    given = jnp.concatenate([theirs, inb[q, s]], axis=0)
                    acc[1, s] += across(given, table)

        r = i - FROM_IN

        @pl.when(is_outer & (r >= 0) & (r < kept))
        def _():
            own = folded(wcat[:, lanes(chunk_at(r), wc)])
            for s in range(steps):
                here = inb.at[r, s]
                along(here, here, outer_z, f_send, in_pos.at[r, s]).wait_recv()
                fin[r, s] = lax.select_n(by_out[s], inb[r, s], own)

        x = i - far_tick

        @pl.when(is_inner & (x >= 0) & (x < PAIR))
        def _():
            @pl.when(x == 0)
            def _():
                along(low, low_x, inner_z, lx_send, lx_sem).wait_recv()

            span = lanes(x, wc)
            d_out[:, span] = jnp.dot(
                low_x[...], both(kept + x), preferred_element_type=F32
            ).astype(BF16)
            for peer in [*partners, me]:
                pltpu.make_async_remote_copy(
                    src_ref=d_out.at[block_rows(peer), span],
                    dst_ref=returned.at[last_place, block_rows(me), span],
                    send_sem=dx_send,
                    recv_sem=d_sem.at[last_place],
                    device_id={"dp": outer_z, "adapter": peer},
                    device_id_type=MESH,
                ).start()

        c = i - plow_tick

        @pl.when((c >= 0) & (c < nw))
        def _():
            @pl.when(lax.rem(c, PAIR) == 0)
            def _():
                wait_exchange(xw_in, c // PAIR, xw_sem)

            low_acc[...] += across(
                xw_in[c // PAIR, :, lanes(lax.rem(c, PAIR), wc)], both(early + c)
            )

        lane = lax.broadcasted_iota(jnp.int32, (cols * cap, steps * rank), 1)

        def per_step(flags):
            return jnp.where(lane < rank, flags[0].astype(jnp.int32), flags[1].astype(jnp.int32)) != 0

        def reduced(k, part):
            out = []
            for s in range(steps):
                x = acc[k, s, part * slots : (part + 1) * slots].reshape(cols, 2, cap, 2 * rank)
                x = [x[:, g].reshape(cols * cap, 2 * rank) for g in range(2)]
                x[1 - s] = pltpu.roll(x[1 - s], rank, axis=1)
                out.append(x[0] + x[1])
            return jnp.where(lane < rank, out[0], out[1])

        @pl.when(is_inner & (i == low_tick))
        def _():
            lm_out[0] = reduced(0, 1).astype(BF16)
            lm_out[1] = reduced(1, 1).astype(BF16)
            lm_out[2] = reduced(1, 0).astype(BF16)
            along(lm_out.at[0], lm_in, mid_z, lm_send, lm_sem).start()
            along(lm_out.at[1], lo_in.at[1], across_z, lm_send, lo_sem.at[1]).start()
            along(lm_out.at[2], lo_in.at[0], outer_z, lm_send, lo_sem.at[0]).start()

        def finish(part):
            spread = jnp.broadcast_to(
                part.reshape(cols, 1, cap, steps * rank), (cols, steps, cap, steps * rank)
            ).reshape(slots, steps * rank)
            of_row = lax.rem(lax.broadcasted_iota(jnp.int32, low.shape, 0), block) // cap
            of_col = lax.broadcasted_iota(jnp.int32, low.shape, 1) // rank
            low[...] = jnp.where(of_row == of_col, low_acc[...] + spread, 0.0).astype(BF16)

        @pl.when(is_inner & (i == done_tick))
        def _():
            along(lm_out.at[0], lm_in, mid_z, lm_send, lm_sem).wait_recv()
            finish(jnp.where(per_step(mine), reduced(0, 0), lm_in[...].astype(F32)))

        @pl.when(is_outer & (i == done_tick))
        def _():
            for k in range(2):
                along(lm_out.at[2 - k], lo_in.at[k], outer_z, lm_send, lo_sem.at[k]).wait_recv()
            theirs = jnp.where(per_step(by_in), lo_in[0].astype(F32), lo_in[1].astype(F32))
            finish(jnp.where(per_step(by_out), reduced(0, 0), theirs))
            along(low, low_x, inner_z, lx_send, lx_sem).start()

        def place(v):
            return lax.rem(v + nd - early // PAIR, nd)

        def deltas(v, c):
            u = v * PAIR + c
            at = u + jnp.where(u < early, 0, nw)
            dout[place(v), :, lanes(c, wc)] = jnp.dot(
                low[...], both(at), preferred_element_type=F32
            ).astype(BF16)

        v = i - done_tick

        @pl.when((v >= 0) & (v < bulk))
        def _():
            for c in range(PAIR):
                deltas(v, c)
            exchange(dout, returned, place(v), pl.ds(0, pw), d_send, d_sem)

        n = i - base_tick

        @pl.when((n >= bulk * PAIR) & (n < count * PAIR))
        def _():
            deltas(n // PAIR, lax.rem(n, PAIR))
            span = lanes(lax.rem(n, PAIR), wc)
            exchange(dout, returned, place(n // PAIR), span, d_send, d_sem)

        def place_rows(e):
            for s in range(steps):
                out_ref[s, :, lanes(e, pw)] = jnp.dot(
                    unpack[s], returned[e], preferred_element_type=F32
                ).astype(BF16)

        def gather(e):
            wait_exchange(returned, e, d_sem)
            place_rows(e)

        v_back = v - OUT_LAG

        @pl.when((v_back >= 0) & (v_back < bulk))
        def _():
            gather(place(v_back))

        n_back = n - OUT_LAG - 1

        @pl.when((n_back >= bulk * PAIR) & (n_back < count * PAIR) & (lax.rem(n_back, PAIR) == 0))
        def _():
            gather(place(n_back // PAIR))

        @pl.when(is_outer & (i == last_tick))
        def _():
            whole = returned.at[last_place]
            pltpu.make_async_copy(whole, whole, d_sem.at[last_place]).wait()
            place_rows(last_place)

        return carry

    lax.fori_loop(0, last_tick + 1, iteration, 0)

    @pl.when(is_outer)
    def _():
        for buf, sem in ((wcat, raw_send), (u_out, u_send), (v_out, v_send), (low, lx_send)):
            pltpu.make_async_copy(buf, buf, sem).wait()
        sent = dout.at[pl.ds(0, nd - 1), pl.ds(0, slots - block)]
        pltpu.make_async_copy(sent, sent, d_send).wait()

    @pl.when(is_inner)
    def _():
        sent = fin.at[pl.ds(0, kept)]
        pltpu.make_async_copy(sent, sent, f_send).wait()
        for buf, sem in ((m_out, m_send), (lm_out, lm_send), (d_out, dx_send)):
            pltpu.make_async_copy(buf, buf, sem).wait()
        sent = dout.at[:, pl.ds(0, slots - block)]
        pltpu.make_async_copy(sent, sent, d_send).wait()

    for buf, sem in ((xt_out, xt_send), (xw_out, xw_send)):
        sent = buf.at[:, pl.ds(0, slots - block)]
        pltpu.make_async_copy(sent, sent, sem).wait()


def split_body(cols, states, request_slot_index, down_weights, up_weights, active_adapter_owner):
    steps, rows, width = states.shape
    rank = down_weights.shape[1]
    cap = 2 * rows // cols
    slots = cols * steps * cap
    wc = WIDTH
    nc = width // wc
    nt = TOKEN_CHUNKS * nc // 64 * 2
    nw = nc - nt
    npos = nw + nc
    early = EARLY
    vmem = pl.BlockSpec(memory_space=pltpu.VMEM)
    hbm = pl.BlockSpec(memory_space=pl.ANY)
    dma = pltpu.SemaphoreType.DMA
    fold = (2 * rank, wc // 2)
    tokens = pltpu.VMEM((nt // PAIR, slots, PAIR * wc), BF16)
    others = pltpu.VMEM((nw // PAIR, slots, PAIR * wc), BF16)
    deltas = pltpu.VMEM((nc // PAIR, slots, PAIR * wc), BF16)
    side = pltpu.VMEM((nt, *fold), BF16)
    stream = pltpu.VMEM((npos, steps, *fold), BF16)
    line = pltpu.VMEM((rank, npos * wc), BF16)
    lows = (cols * cap, steps * rank)
    return pl.pallas_call(
        functools.partial(split_kernel, cols, steps, cap, wc, nt, early),
        out_shape=pltpu.VMEM(states.shape, states.dtype),
        in_specs=[pl.BlockSpec(memory_space=pltpu.SMEM), vmem, hbm, hbm, hbm],
        out_specs=vmem,
        scratch_shapes=[
            pltpu.VMEM(states.shape, BF16),
            pltpu.VMEM((rank, nt * wc), BF16),
            line, line, side, side, side, side, stream, stream, stream,
            tokens, tokens, others, others, deltas, deltas,
            pltpu.VMEM((2, steps, 2 * slots, 2 * rank), F32),
            pltpu.VMEM((slots, steps * rank), F32),
            pltpu.VMEM((slots, steps * rank), BF16),
            pltpu.VMEM((slots, steps * rank), BF16),
            pltpu.VMEM((slots, PAIR * wc), BF16),
            pltpu.VMEM((3, *lows), BF16), pltpu.VMEM(lows, BF16), pltpu.VMEM((2, *lows), BF16),
            pltpu.VMEM((steps, 2, slots, rows), BF16),
            pltpu.VMEM((steps, slots, rows), BF16),
            pltpu.VMEM((steps, rows, slots), BF16),
            dma((4,)), dma, dma, dma, dma, dma, dma, dma, dma, dma, dma, dma,
            dma((npos,)), dma((nt,)), dma((nt,)), dma((npos, steps)),
            dma((nt // PAIR,)), dma((nw // PAIR,)), dma((nc // PAIR,)), dma, dma((2,)), dma,
        ],
        compiler_params=pltpu.CompilerParams(
            collective_id=0, has_side_effects=True, vmem_limit_bytes=56 * 1024 * 1024
        ),
    )(active_adapter_owner, request_slot_index[:, :, 0], states, down_weights, up_weights)


def routed(n, cols, states, request_slot_index, down_weights, up_weights, active_adapter_owner):
    steps, rows, width = states.shape
    cap = 2 * rows // cols
    paired = steps == 2 and cap == 8 and cols * cap == down_weights.shape[1]
    if n == 4 and paired and width % (8 * WIDTH) == 0:
        run = functools.partial(split_body, cols)
    else:
        run = functools.partial(body, n, cols)
    return run(states, request_slot_index, down_weights, up_weights, active_adapter_owner)


def solution(mesh):
    return jax.shard_map(
        functools.partial(routed, mesh.shape["dp"], mesh.shape["adapter"]),
        mesh=mesh,
        in_specs=(
            P(None, ("dp", "adapter"), None),
            P(None, ("dp", "adapter"), None),
            P(("dp", "adapter"), None, None),
            P(("dp", "adapter"), None, None),
            P(),
        ),
        out_specs=P(None, ("dp", "adapter"), None),
        check_vma=False,
    )
```

```python
import functools

import jax
import jax.numpy as jnp
from jax import lax
from jax.experimental import pallas as pl
from jax.experimental.pallas import tpu as pltpu
from jax.sharding import PartitionSpec as P

MESH = pl.DeviceIdType.MESH
F32 = jnp.float32
BF16 = jnp.bfloat16
WIDTH = 256
SKEW = 3
LAG = 3
GROUP = 2


def kernel(
    n, cols, steps, cap, block, wc, group,
    owner_ref, slot_ref, states_any, down_any, up_any, out_ref,
    states_ref, down_ref, up_ref, below, above, xout, arrived, dout, returned, low_acc, low, pack, unpack,
    in_sem, up_send, dn_send, x_send, d_send, below_sem, above_sem, x_sem, d_sem,
):
    z = lax.axis_index("dp")
    me = lax.axis_index("adapter")
    rows = states_any.shape[1]
    rank = down_any.shape[1]
    nw = states_any.shape[2] // wc
    nch = 2 * nw
    slots = cols * block
    not_first = z > 0
    not_last = z < n - 1

    pieces = nw // group
    pw = wc * group
    loads = [
        pltpu.make_async_copy(src, dst, in_sem.at[i])
        for i, (src, dst) in enumerate(
            ((down_any, down_ref), (up_any, up_ref), (states_any, states_ref))
        )
    ]
    for load in loads:
        load.start()

    def lanes(w):
        return pl.ds(pl.multiple_of(w * wc, wc), wc)

    def piece_lanes(p):
        return pl.ds(pl.multiple_of(p * pw, pw), pw)

    def block_rows(j):
        return pl.ds(pl.multiple_of(j * block, block), block)

    barrier = pltpu.get_barrier_semaphore()
    for o in range(1, cols):
        pl.semaphore_signal(
            barrier, inc=1, device_id={"adapter": lax.rem(me + o, cols)}, device_id_type=MESH
        )

    @pl.when(not_first)
    def _():
        pl.semaphore_signal(barrier, inc=1, device_id={"dp": z - 1}, device_id_type=MESH)

    @pl.when(not_last)
    def _():
        pl.semaphore_signal(barrier, inc=1, device_id={"dp": z + 1}, device_id_type=MESH)

    r_sub = lax.broadcasted_iota(jnp.int32, (rows, rows), 0)
    r_lane = lax.broadcasted_iota(jnp.int32, (rows, rows), 1)
    for s in range(steps):
        crow = slot_ref[s : s + 1, :]
        crow_b = jnp.broadcast_to(crow, (rows, rows))
        ccol = jnp.sum(jnp.where(r_sub == r_lane, crow_b, 0), axis=1, keepdims=True)
        same = jnp.broadcast_to(ccol, (rows, rows)) == crow_b
        rank_row = jnp.sum(jnp.where(same & (r_sub < r_lane), 1, 0), axis=0, keepdims=True)
        rank_col = jnp.sum(jnp.where(same & (r_lane < r_sub), 1, 0), axis=1, keepdims=True)
        trow = crow * block + s * cap + rank_row
        tcol = ccol * block + s * cap + rank_col
        pack[s] = jnp.where(
            lax.broadcasted_iota(jnp.int32, (slots, rows), 0) == trow, 1.0, 0.0
        ).astype(BF16)
        unpack[s] = jnp.where(
            lax.broadcasted_iota(jnp.int32, (rows, slots), 1) == tcol, 1.0, 0.0
        ).astype(BF16)
    low_acc[...] = jnp.zeros_like(low_acc)

    owners = [owner_ref[s, me] for s in range(steps)]
    for load in loads:
        load.wait()
    pl.semaphore_wait(
        barrier, cols - 1 + not_first.astype(jnp.int32) + not_last.astype(jnp.int32)
    )

    def own(k, use):
        @pl.when(k < nw)
        def _():
            use(down_ref[0, :, lanes(k)])

        @pl.when(k >= nw)
        def _():
            use(up_ref[0, :, lanes(k - nw)])

    def part(s):
        return pl.ds(s * rank, rank)

    def hop(buf, i, place, owner_places, target, recv_sem, send_sem):
        def copy(k, src, dst):
            return pltpu.make_async_remote_copy(
                src_ref=buf.at[k, src],
                dst_ref=buf.at[k, dst],
                send_sem=send_sem,
                recv_sem=recv_sem.at[k],
                device_id={"dp": target},
                device_id_type=MESH,
            )

        whole = pl.ds(0, steps * rank)
        second = i - SKEW
        later = i - SKEW * place

        @pl.when((place == 0) & (i < nch))
        def _():
            def use(mine):
                for s in range(steps):
                    buf[i, part(s), :] = mine

            own(i, use)
            copy(i, part(0), part(1)).start()

        @pl.when((place == 1) & (i < nch))
        def _():
            def use(mine):
                buf[i, part(0), :] = mine

            own(i, use)

            @pl.when(place < n - 1)
            def _():
                copy(i, part(0), part(0)).start()

        @pl.when((place == 1) & (second >= 0) & (second < nch))
        def _():
            copy(second, part(1), part(1)).wait_recv()

            @pl.when(place < n - 1)
            def _():
                copy(second, part(1), part(1)).start()

        @pl.when((place > 1) & (later >= 0) & (later < nch))
        def _():
            copy(later, whole, whole).wait_recv()

            def use(mine):
                theirs = [buf[later, part(s), :] for s in range(steps)]
                for s in range(steps):
                    value = theirs[s]
                    raw = place == 2
                    if s == 0:
                        value = lax.select_n(raw & (owner_places[s] == 0), value, theirs[1])
                    else:
                        value = lax.select_n(raw & (owner_places[s] == 0), value, theirs[1])
                        value = lax.select_n(raw & (owner_places[s] == 1), value, theirs[0])
                    buf[later, part(s), :] = lax.select_n(owner_places[s] == place, value, mine)

            own(later, use)

            @pl.when(place < n - 1)
            def _():
                copy(later, whole, whole).start()

    def wait_sent(buf, place, send_sem):
        @pl.when(place == 0)
        def _():
            sent = buf.at[:, part(0)]
            pltpu.make_async_copy(sent, sent, send_sem).wait()

        @pl.when((place > 0) & (place < n - 1))
        def _():
            pltpu.make_async_copy(buf, buf, send_sem).wait()

    partners = []
    for o in range(cols - 1, 0, -1):
        peer, bit = 0, 1
        while bit < cols:
            peer = peer + bit * lax.rem(lax.rem(me // bit, 2) + o // bit % 2, 2)
            bit = 2 * bit
        partners.append(peer if bit == cols else lax.rem(me + o, cols))

    def exchange(src, dst, w, span, send_sem, recv_sem):
        for peer in partners:
            pltpu.make_async_remote_copy(
                src_ref=src.at[w, block_rows(peer), span],
                dst_ref=dst.at[w, block_rows(me), span],
                send_sem=send_sem,
                recv_sem=recv_sem.at[w],
                device_id={"adapter": peer},
                device_id_type=MESH,
            ).start()
        dst[w, block_rows(me), span] = src[w, block_rows(me), span]

    def wait_exchange(dst, w, recv_sem):
        remote = dst.at[w, pl.ds(0, slots - block)]
        pltpu.make_async_copy(remote, remote, recv_sem.at[w]).wait()

    ups = owners
    dns = [n - 1 - owner for owner in owners]

    def pick(buf, k, place, owner_places, s):
        other = (place == 1) & (owner_places[s] == (0 if s == 0 else 1))
        return lax.select_n(other, buf[k, part(s), :], buf[k, part(1 if s == 0 else 0), :])

    def chosen(k):
        parts = []
        for s in range(steps):
            parts.append(
                lax.select_n(
                    owners[s] <= z,
                    pick(above, k, n - 1 - z, dns, s),
                    pick(below, k, z, ups, s),
                )
            )
        return jnp.concatenate(parts, axis=0)

    def iteration(i, carry):
        hop(below, i, z, ups, lax.rem(z + 1, n), below_sem, up_send)
        hop(above, i, n - 1 - z, dns, lax.rem(z + n - 1, n), above_sem, dn_send)

        @pl.when((lax.rem(i, group) == 0) & (i < nw))
        def _():
            p = i // group
            total = jnp.zeros((slots, pw), F32)
            for s in range(steps):
                total = total + jnp.dot(
                    pack[s], states_ref[s, :, piece_lanes(p)], preferred_element_type=F32
                )
            xout[p] = total.astype(BF16)
            exchange(xout, arrived, p, pl.ds(0, pw), x_send, x_sem)

        k = i - SKEW * (n - 1)

        @pl.when((k >= 0) & (k < nw) & (lax.rem(k, group) == 0))
        def _():
            wait_exchange(arrived, k // group, x_sem)

        @pl.when((k >= 0) & (k < nw))
        def _():
            low_acc[...] += lax.dot_general(
                arrived[k // group, :, lanes(lax.rem(k, group))],
                chosen(k),
                (((1,), (1,)), ((), ())),
                preferred_element_type=F32,
            )

        @pl.when(k == nw - 1)
        def _():
            of_row = lax.rem(lax.broadcasted_iota(jnp.int32, low.shape, 0), block) // cap
            of_col = lax.broadcasted_iota(jnp.int32, low.shape, 1) // rank
            low[...] = jnp.where(of_row == of_col, low_acc[...], 0.0).astype(BF16)

        @pl.when((k >= nw) & (k < nch))
        def _():
            w = k - nw
            dout[w // group, :, lanes(lax.rem(w, group))] = jnp.dot(
                low[...], chosen(k), preferred_element_type=F32
            ).astype(BF16)

        @pl.when((k >= nw) & (k < nch - group) & (lax.rem(k - nw, group) == group - 1))
        def _():
            exchange(dout, returned, (k - nw) // group, pl.ds(0, pw), d_send, d_sem)

        @pl.when((k >= nch - group) & (k < nch))
        def _():
            span = lanes(lax.rem(k - nw, group))
            exchange(dout, returned, pieces - 1, span, d_send, d_sem)

        w_out = k - nw - LAG

        @pl.when((w_out >= 0) & (w_out < nw) & (lax.rem(w_out, group) == group - 1))
        def _():
            p = w_out // group
            wait_exchange(returned, p, d_sem)
            for s in range(steps):
                out_ref[s, :, piece_lanes(p)] = jnp.dot(
                    unpack[s], returned[p], preferred_element_type=F32
                ).astype(BF16)

        return carry

    lax.fori_loop(0, nch + SKEW * (n - 1) + LAG, iteration, 0)

    wait_sent(below, z, up_send)
    wait_sent(above, n - 1 - z, dn_send)
    for buf, sem in ((xout, x_send), (dout, d_send)):
        sent = buf.at[:, pl.ds(0, slots - block)]
        pltpu.make_async_copy(sent, sent, sem).wait()


def body(n, cols, states, request_slot_index, down_weights, up_weights, active_adapter_owner):
    steps, rows, width = states.shape
    rank = down_weights.shape[1]
    cap = max(2, 2 * rows // cols)
    block = -(-steps * cap // 16) * 16
    slots = cols * block
    wc = min(WIDTH, width)
    nw = width // wc
    group = GROUP if nw % GROUP == 0 else 1
    vmem = pl.BlockSpec(memory_space=pltpu.VMEM)
    hbm = pl.BlockSpec(memory_space=pl.ANY)
    dma = pltpu.SemaphoreType.DMA
    stream = pltpu.VMEM((2 * nw, steps * rank, wc), BF16)
    piece = pltpu.VMEM((nw // group, slots, wc * group), BF16)
    return pl.pallas_call(
        functools.partial(kernel, n, cols, steps, cap, block, wc, group),
        out_shape=pltpu.VMEM(states.shape, states.dtype),
        in_specs=[pl.BlockSpec(memory_space=pltpu.SMEM), vmem, hbm, hbm, hbm],
        out_specs=vmem,
        scratch_shapes=[
            pltpu.VMEM(states.shape, BF16),
            pltpu.VMEM(down_weights.shape, BF16),
            pltpu.VMEM(up_weights.shape, BF16),
            stream, stream, piece, piece, piece, piece,
            pltpu.VMEM((slots, steps * rank), F32),
            pltpu.VMEM((slots, steps * rank), BF16),
            pltpu.VMEM((steps, slots, rows), BF16),
            pltpu.VMEM((steps, rows, slots), BF16),
            dma((3,)), dma, dma, dma, dma,
            dma((2 * nw,)), dma((2 * nw,)), dma((nw // group,)), dma((nw // group,)),
        ],
        compiler_params=pltpu.CompilerParams(
            collective_id=0, has_side_effects=True, vmem_limit_bytes=56 * 1024 * 1024
        ),
    )(active_adapter_owner, request_slot_index[:, :, 0], states, down_weights, up_weights)


TOKEN_CHUNKS = 14
EARLY = 4
PAIR = 2
TO_MID, FROM_MID, FROM_IN = 2, 5, 8
OUT_LAG = 5
FAR_PIECES = 2
DONE_IN, DONE_OUT = 3, 3


def split_kernel(
    cols, steps, cap, wc, nt, early,
    owner_ref, slot_ref, states_any, down_any, up_any, out_ref,
    states_ref, dt, wcat, raw, u_out, v_out, u_in, v_in, m_out, inb, fin,
    xt_out, xt_in, xw_out, xw_in, dout, returned,
    acc, low_acc, low, low_x, d_out, lm_out, lm_in, lo_in, pack_t, pack_w, unpack,
    in_sem, raw_send, u_send, v_send, m_send, f_send, xt_send, xw_send, d_send, lm_send, lx_send, dx_send,
    raw_sem, u_sem, v_sem, in_pos, xt_sem, xw_sem, d_sem, lm_sem, lo_sem, lx_sem,
):
    z = lax.axis_index("dp")
    me = lax.axis_index("adapter")
    rows, width = states_any.shape[1:]
    rank = down_any.shape[1]
    block = steps * cap
    slots = cols * block
    half = wc // 2
    nc = width // wc
    nw = nc - nt
    npos = nw + nc
    pw = PAIR * wc
    nd = nc // PAIR
    low_tick = early + 2 * nt + FROM_MID - 1
    roles = [(low_tick + DONE_IN, nw + FROM_MID), (low_tick + DONE_OUT, nw + FROM_IN)]
    counts = [nd, nd - FAR_PIECES]
    bulks = [min(max(done - base, 0), n) for (done, base), n in zip(roles, counts)]
    ends = [
        max(done + bulk, base + 2 * n) if bulk < n else done + bulk
        for (done, base), bulk, n in zip(roles, bulks, counts)
    ]
    last_tick = max(ends) + OUT_LAG
    far_place = nd - FAR_PIECES - early // PAIR
    kept = npos - FAR_PIECES * PAIR
    far_tick = max(kept + FROM_MID, roles[1][0] + 1)
    plow_tick = early + FROM_IN + nt // 2
    xw_tick = nt // PAIR

    far = z // 2
    is_outer = (z == 0) | (z == 3)
    is_inner = (z == 1) | (z == 2)
    inner_z = 1 + far
    outer_z = 3 * far
    mid_z = 2 - far
    across_z = jnp.where(is_inner, 3 - outer_z, 3 - inner_z)
    done_tick = jnp.where(is_inner, roles[0][0], roles[1][0])
    base_tick = jnp.where(is_inner, roles[0][1], roles[1][1])
    bulk = jnp.where(is_inner, bulks[0], bulks[1])
    count = jnp.where(is_inner, counts[0], counts[1])

    owners = [owner_ref[s, me] for s in range(steps)]
    by_in = [a == inner_z for a in owners]
    by_out = [a == outer_z for a in owners]
    mine = [i | o for i, o in zip(by_in, by_out)]
    any_out = by_out[0] | by_out[1]

    def lanes(k, n):
        return pl.ds(pl.multiple_of(k * n, n), n)

    def block_rows(j):
        return pl.ds(pl.multiple_of(j * block, block), block)

    tw = nt * wc
    loads = [
        pltpu.make_async_copy(src, dst, in_sem.at[i])
        for i, (src, dst) in enumerate(
            (
                (states_any, states_ref),
                (up_any.at[0], wcat.at[:, pl.ds(nw * wc, width)]),
                (down_any.at[0, :, pl.ds(tw, nw * wc)], wcat.at[:, pl.ds(0, nw * wc)]),
                (down_any.at[0, :, pl.ds(0, tw)], dt),
            )
        )
    ]
    for load in loads:
        load.start()

    barrier = pltpu.get_barrier_semaphore()
    for o in range(1, cols):
        pl.semaphore_signal(
            barrier, inc=1, device_id={"adapter": lax.rem(me + o, cols)}, device_id_type=MESH
        )

    pl.semaphore_signal(barrier, inc=1, device_id={"dp": across_z}, device_id_type=MESH)

    @pl.when(is_outer)
    def _():
        for o in range(1, cols):
            pl.semaphore_signal(
                barrier,
                inc=1,
                device_id={"dp": inner_z, "adapter": lax.rem(me + o, cols)},
                device_id_type=MESH,
            )

    @pl.when(z > 0)
    def _():
        pl.semaphore_signal(barrier, inc=1, device_id={"dp": z - 1}, device_id_type=MESH)

    @pl.when(z < 3)
    def _():
        pl.semaphore_signal(barrier, inc=1, device_id={"dp": z + 1}, device_id_type=MESH)

    r_sub = lax.broadcasted_iota(jnp.int32, (rows, rows), 0)
    r_lane = lax.broadcasted_iota(jnp.int32, (rows, rows), 1)
    for s in range(steps):
        crow = slot_ref[s : s + 1, :]
        crow_b = jnp.broadcast_to(crow, (rows, rows))
        ccol = jnp.sum(jnp.where(r_sub == r_lane, crow_b, 0), axis=1, keepdims=True)
        same = jnp.broadcast_to(ccol, (rows, rows)) == crow_b
        rank_row = jnp.sum(jnp.where(same & (r_sub < r_lane), 1, 0), axis=0, keepdims=True)
        rank_col = jnp.sum(jnp.where(same & (r_lane < r_sub), 1, 0), axis=1, keepdims=True)
        at = lax.broadcasted_iota(jnp.int32, (slots, rows), 0)
        for g in range(2):
            pack_t[s, g] = jnp.where(at == crow * block + g * cap + rank_row, 1.0, 0.0).astype(BF16)
        pack_w[s] = jnp.where(at == crow * block + s * cap + rank_row, 1.0, 0.0).astype(BF16)
        unpack[s] = jnp.where(
            lax.broadcasted_iota(jnp.int32, (rows, slots), 1) == ccol * block + s * cap + rank_col,
            1.0,
            0.0,
        ).astype(BF16)
    low_acc[...] = jnp.zeros_like(low_acc)
    acc[...] = jnp.zeros_like(acc)

    for load in loads:
        load.wait()
    pl.semaphore_wait(barrier, cols + jnp.where(is_inner, cols + 1, 1))

    partners = []
    for o in range(cols - 1, 0, -1):
        peer, bit = 0, 1
        while bit < cols:
            peer = peer + bit * lax.rem(lax.rem(me // bit, 2) + o // bit % 2, 2)
            bit = 2 * bit
        partners.append(peer if bit == cols else lax.rem(me + o, cols))

    def exchange(src, dst, w, span, send_sem, recv_sem):
        for peer in partners:
            pltpu.make_async_remote_copy(
                src_ref=src.at[w, block_rows(peer), span],
                dst_ref=dst.at[w, block_rows(me), span],
                send_sem=send_sem,
                recv_sem=recv_sem.at[w],
                device_id={"adapter": peer},
                device_id_type=MESH,
            ).start()
        dst[w, block_rows(me), span] = src[w, block_rows(me), span]

    def wait_exchange(dst, w, recv_sem):
        remote = dst.at[w, pl.ds(0, slots - block)]
        pltpu.make_async_copy(remote, remote, recv_sem.at[w]).wait()

    def along(src, dst, target, send_sem, recv_sem):
        return pltpu.make_async_remote_copy(
            src_ref=src,
            dst_ref=dst,
            send_sem=send_sem,
            recv_sem=recv_sem,
            device_id={"dp": target},
            device_id_type=MESH,
        )

    def folded(x):
        return jnp.concatenate([x[:, :half], x[:, half:]], axis=0)

    def unfolded(x):
        return jnp.concatenate([x[:rank], x[rank:]], axis=1)

    def across(a, b):
        return lax.dot_general(a, b, (((1,), (1,)), ((), ())), preferred_element_type=F32)

    def token(t, s):
        return xt_in[t // PAIR, :, lanes(s * PAIR + lax.rem(t, PAIR), half)]

    def chunk_at(p):
        return lax.rem(p + npos - early, npos)

    def both(p):
        return jnp.concatenate([unfolded(fin[p, s]) for s in range(steps)], axis=0)

    def known(w):
        own = folded(wcat[:, lanes(w, wc)])
        theirs = folded(raw[:, lanes(w, wc)])
        return [lax.select_n(by_in[s], theirs, own) for s in range(steps)]

    def iteration(i, carry):
        @pl.when(is_outer & (i < npos))
        def _():
            w = chunk_at(i)
            along(
                wcat.at[:, lanes(w, wc)], raw.at[:, lanes(w, wc)], inner_z, raw_send, raw_sem.at[w]
            ).start()

        @pl.when(i < nt // PAIR)
        def _():
            for s in range(steps):
                packs = jnp.concatenate([pack_t[s, g] for g in range(2)], axis=1)
                parts = []
                for c in range(PAIR):
                    wide = states_ref[s, :, lanes(i * PAIR + c, wc)]
                    parts.append(jnp.concatenate([wide[:, :half], wide[:, half:]], axis=0))
                xt_out[i, :, pl.ds(s * PAIR * half, PAIR * half)] = jnp.dot(
                    packs, jnp.concatenate(parts, axis=1), preferred_element_type=F32
                ).astype(BF16)
            exchange(xt_out, xt_in, i, pl.ds(0, pw), xt_send, xt_sem)

        a = i - xw_tick

        @pl.when((a >= 0) & (a < nw // PAIR))
        def _():
            packs = jnp.concatenate([pack_w[s] for s in range(steps)], axis=1)
            wide = jnp.concatenate(
                [states_ref[s, :, lanes(nt // PAIR + a, pw)] for s in range(steps)], axis=0
            )
            xw_out[a] = jnp.dot(packs, wide, preferred_element_type=F32).astype(BF16)
            exchange(xw_out, xw_in, a, pl.ds(0, pw), xw_send, xw_sem)

        @pl.when(is_outer & (i < npos))
        def _():
            t = i - early

            @pl.when((t >= 0) & (t < nt))
            def _():
                @pl.when(lax.rem(t, PAIR) == 0)
                def _():
                    wait_exchange(xt_in, t // PAIR, xt_sem)

                mine_t = folded(dt[:, lanes(t, wc)])
                u_out[t] = lax.select_n(any_out, token(t, 0), mine_t)
                along(u_out.at[t], u_in.at[t], inner_z, u_send, u_sem.at[t]).start()
                v_out[t] = lax.select_n(by_out[1], token(t, 1), token(t, 0))
                for s in range(steps):
                    acc[0, s, 0:slots] += across(token(t, s), mine_t)

            @pl.when((t >= nt) & (t < 2 * nt))
            def _():
                along(v_out.at[t - nt], v_in.at[t - nt], inner_z, v_send, v_sem.at[t - nt]).start()

        p = i - TO_MID

        @pl.when(is_inner & (p >= 0) & (p < npos))
        def _():
            w = chunk_at(p)
            theirs = raw.at[:, lanes(w, wc)]
            along(theirs, theirs, inner_z, raw_send, raw_sem.at[w]).wait_recv()
            weights = known(w)
            t = p - early

            @pl.when((t < 0) | (t >= 2 * nt))
            def _():
                for s in range(steps):
                    m_out[p, s] = weights[s]

            @pl.when((t >= 0) & (t < nt))
            def _():
                @pl.when(lax.rem(t, PAIR) == 0)
                def _():
                    wait_exchange(xt_in, t // PAIR, xt_sem)

                for s in range(steps):
                    m_out[p, s] = lax.select_n(mine[s], token(t, s), weights[s])

            @pl.when((t >= nt) & (t < 2 * nt))
            def _():
                v = t - nt
                along(v_out.at[v], v_in.at[v], inner_z, v_send, v_sem.at[v]).wait_recv()
                first = lax.select_n(by_out[1], u_in[v], v_in[v])
                m_out[p, 0] = lax.select_n(mine[0], first, weights[0])
                m_out[p, 1] = lax.select_n(mine[1], v_in[v], weights[1])

            for s in range(steps):
                along(m_out.at[p, s], inb.at[p, s], mid_z, m_send, in_pos.at[p, s]).start()

        q = i - FROM_MID

        @pl.when(is_inner & (q >= 0) & (q < npos))
        def _():
            weights = known(chunk_at(q))
            for s in range(steps):
                here = inb.at[q, s]
                along(here, here, mid_z, m_send, in_pos.at[q, s]).wait_recv()
                fin[q, s] = lax.select_n(mine[s], inb[q, s], weights[s])

                @pl.when(q < kept)
                def _():
                    along(fin.at[q, s], here, outer_z, f_send, in_pos.at[q, s]).start()

            t = q - early

            @pl.when((t >= 0) & (t < nt))
            def _():
                along(u_out.at[t], u_in.at[t], inner_z, u_send, u_sem.at[t]).wait_recv()
                mine_t = folded(dt[:, lanes(t, wc)])
                for s in range(steps):
                    table = lax.select_n(by_out[s], mine_t, u_in[t])
                    given = jnp.concatenate([token(t, s), inb[q, s]], axis=0)
                    acc[0, s] += across(given, table)

            @pl.when((t >= nt) & (t < 2 * nt))
            def _():
                v = t - nt
                mine_t = folded(dt[:, lanes(v, wc)])
                for s in range(steps):
                    table = lax.select_n(by_out[s], mine_t, u_in[v])
                    theirs = v_in[v]
                    if s == 0:
                        theirs = lax.select_n(by_out[1], u_in[v], theirs)
                    given = jnp.concatenate([theirs, inb[q, s]], axis=0)
                    acc[1, s] += across(given, table)

        r = i - FROM_IN

        @pl.when(is_outer & (r >= 0) & (r < kept))
        def _():
            own = folded(wcat[:, lanes(chunk_at(r), wc)])
            for s in range(steps):
                here = inb.at[r, s]
                along(here, here, outer_z, f_send, in_pos.at[r, s]).wait_recv()
                fin[r, s] = lax.select_n(by_out[s], inb[r, s], own)

        x = i - far_tick

        @pl.when(is_inner & (x >= 0) & (x < FAR_PIECES * PAIR))
        def _():
            @pl.when(x == 0)
            def _():
                along(low, low_x, inner_z, lx_send, lx_sem).wait_recv()

            k = x // PAIR
            span = lanes(lax.rem(x, PAIR), wc)
            d_out[k, :, span] = jnp.dot(
                low_x[...], both(kept + x), preferred_element_type=F32
            ).astype(BF16)
            for peer in [*partners, me]:
                pltpu.make_async_remote_copy(
                    src_ref=d_out.at[k, block_rows(peer), span],
                    dst_ref=returned.at[far_place + k, block_rows(me), span],
                    send_sem=dx_send,
                    recv_sem=d_sem.at[far_place + k],
                    device_id={"dp": outer_z, "adapter": peer},
                    device_id_type=MESH,
                ).start()

        c = i - plow_tick

        @pl.when((c >= 0) & (c < nw))
        def _():
            @pl.when(lax.rem(c, PAIR) == 0)
            def _():
                wait_exchange(xw_in, c // PAIR, xw_sem)

            low_acc[...] += across(
                xw_in[c // PAIR, :, lanes(lax.rem(c, PAIR), wc)], both(early + c)
            )

        lane = lax.broadcasted_iota(jnp.int32, (cols * cap, steps * rank), 1)

        def per_step(flags):
            return jnp.where(lane < rank, flags[0].astype(jnp.int32), flags[1].astype(jnp.int32)) != 0

        def reduced(k, part):
            out = []
            for s in range(steps):
                x = acc[k, s, part * slots : (part + 1) * slots].reshape(cols, 2, cap, 2 * rank)
                x = [x[:, g].reshape(cols * cap, 2 * rank) for g in range(2)]
                x[1 - s] = pltpu.roll(x[1 - s], rank, axis=1)
                out.append(x[0] + x[1])
            return jnp.where(lane < rank, out[0], out[1])

        @pl.when(is_inner & (i == low_tick))
        def _():
            lm_out[0] = reduced(0, 1).astype(BF16)
            lm_out[1] = reduced(1, 1).astype(BF16)
            lm_out[2] = reduced(1, 0).astype(BF16)
            along(lm_out.at[0], lm_in, mid_z, lm_send, lm_sem).start()
            along(lm_out.at[1], lo_in.at[1], across_z, lm_send, lo_sem.at[1]).start()
            along(lm_out.at[2], lo_in.at[0], outer_z, lm_send, lo_sem.at[0]).start()

        def finish(part):
            spread = jnp.broadcast_to(
                part.reshape(cols, 1, cap, steps * rank), (cols, steps, cap, steps * rank)
            ).reshape(slots, steps * rank)
            of_row = lax.rem(lax.broadcasted_iota(jnp.int32, low.shape, 0), block) // cap
            of_col = lax.broadcasted_iota(jnp.int32, low.shape, 1) // rank
            low[...] = jnp.where(of_row == of_col, low_acc[...] + spread, 0.0).astype(BF16)

        @pl.when(is_inner & (i == done_tick))
        def _():
            along(lm_out.at[0], lm_in, mid_z, lm_send, lm_sem).wait_recv()
            finish(jnp.where(per_step(mine), reduced(0, 0), lm_in[...].astype(F32)))

        @pl.when(is_outer & (i == done_tick))
        def _():
            for k in range(2):
                along(lm_out.at[2 - k], lo_in.at[k], outer_z, lm_send, lo_sem.at[k]).wait_recv()
            theirs = jnp.where(per_step(by_in), lo_in[0].astype(F32), lo_in[1].astype(F32))
            finish(jnp.where(per_step(by_out), reduced(0, 0), theirs))
            along(low, low_x, inner_z, lx_send, lx_sem).start()

        def place(v):
            return lax.rem(v + nd - early // PAIR, nd)

        def deltas(v, c):
            u = v * PAIR + c
            at = u + jnp.where(u < early, 0, nw)
            dout[place(v), :, lanes(c, wc)] = jnp.dot(
                low[...], both(at), preferred_element_type=F32
            ).astype(BF16)

        v = i - done_tick

        @pl.when((v >= 0) & (v < bulk))
        def _():
            for c in range(PAIR):
                deltas(v, c)
            exchange(dout, returned, place(v), pl.ds(0, pw), d_send, d_sem)

        n = i - base_tick

        @pl.when((n >= bulk * PAIR) & (n < count * PAIR))
        def _():
            deltas(n // PAIR, lax.rem(n, PAIR))
            span = lanes(lax.rem(n, PAIR), wc)
            exchange(dout, returned, place(n // PAIR), span, d_send, d_sem)

        def place_rows(e):
            for s in range(steps):
                out_ref[s, :, lanes(e, pw)] = jnp.dot(
                    unpack[s], returned[e], preferred_element_type=F32
                ).astype(BF16)

        def gather(e):
            wait_exchange(returned, e, d_sem)
            place_rows(e)

        v_back = v - OUT_LAG

        @pl.when((v_back >= 0) & (v_back < bulk))
        def _():
            gather(place(v_back))

        n_back = n - OUT_LAG - 1

        @pl.when((n_back >= bulk * PAIR) & (n_back < count * PAIR) & (lax.rem(n_back, PAIR) == 0))
        def _():
            gather(place(n_back // PAIR))

        @pl.when(is_outer & (i == last_tick))
        def _():
            for k in range(FAR_PIECES):
                whole = returned.at[far_place + k]
                pltpu.make_async_copy(whole, whole, d_sem.at[far_place + k]).wait()
                place_rows(far_place + k)

        return carry

    lax.fori_loop(0, last_tick + 1, iteration, 0)

    @pl.when(is_outer)
    def _():
        for buf, sem in ((wcat, raw_send), (u_out, u_send), (v_out, v_send), (low, lx_send)):
            pltpu.make_async_copy(buf, buf, sem).wait()
        sent = dout.at[pl.ds(0, nd - FAR_PIECES), pl.ds(0, slots - block)]
        pltpu.make_async_copy(sent, sent, d_send).wait()

    @pl.when(is_inner)
    def _():
        sent = fin.at[pl.ds(0, kept)]
        pltpu.make_async_copy(sent, sent, f_send).wait()
        for buf, sem in ((m_out, m_send), (lm_out, lm_send), (d_out, dx_send)):
            pltpu.make_async_copy(buf, buf, sem).wait()
        sent = dout.at[:, pl.ds(0, slots - block)]
        pltpu.make_async_copy(sent, sent, d_send).wait()

    for buf, sem in ((xt_out, xt_send), (xw_out, xw_send)):
        sent = buf.at[:, pl.ds(0, slots - block)]
        pltpu.make_async_copy(sent, sent, sem).wait()


def split_body(cols, states, request_slot_index, down_weights, up_weights, active_adapter_owner):
    steps, rows, width = states.shape
    rank = down_weights.shape[1]
    cap = 2 * rows // cols
    slots = cols * steps * cap
    wc = WIDTH
    nc = width // wc
    nt = TOKEN_CHUNKS * nc // 64 * 2
    nw = nc - nt
    npos = nw + nc
    early = EARLY
    vmem = pl.BlockSpec(memory_space=pltpu.VMEM)
    hbm = pl.BlockSpec(memory_space=pl.ANY)
    dma = pltpu.SemaphoreType.DMA
    fold = (2 * rank, wc // 2)
    tokens = pltpu.VMEM((nt // PAIR, slots, PAIR * wc), BF16)
    others = pltpu.VMEM((nw // PAIR, slots, PAIR * wc), BF16)
    deltas = pltpu.VMEM((nc // PAIR, slots, PAIR * wc), BF16)
    side = pltpu.VMEM((nt, *fold), BF16)
    stream = pltpu.VMEM((npos, steps, *fold), BF16)
    line = pltpu.VMEM((rank, npos * wc), BF16)
    lows = (cols * cap, steps * rank)
    return pl.pallas_call(
        functools.partial(split_kernel, cols, steps, cap, wc, nt, early),
        out_shape=pltpu.VMEM(states.shape, states.dtype),
        in_specs=[pl.BlockSpec(memory_space=pltpu.SMEM), vmem, hbm, hbm, hbm],
        out_specs=vmem,
        scratch_shapes=[
            pltpu.VMEM(states.shape, BF16),
            pltpu.VMEM((rank, nt * wc), BF16),
            line, line, side, side, side, side, stream, stream, stream,
            tokens, tokens, others, others, deltas, deltas,
            pltpu.VMEM((2, steps, 2 * slots, 2 * rank), F32),
            pltpu.VMEM((slots, steps * rank), F32),
            pltpu.VMEM((slots, steps * rank), BF16),
            pltpu.VMEM((slots, steps * rank), BF16),
            pltpu.VMEM((FAR_PIECES, slots, PAIR * wc), BF16),
            pltpu.VMEM((3, *lows), BF16), pltpu.VMEM(lows, BF16), pltpu.VMEM((2, *lows), BF16),
            pltpu.VMEM((steps, 2, slots, rows), BF16),
            pltpu.VMEM((steps, slots, rows), BF16),
            pltpu.VMEM((steps, rows, slots), BF16),
            dma((4,)), dma, dma, dma, dma, dma, dma, dma, dma, dma, dma, dma,
            dma((npos,)), dma((nt,)), dma((nt,)), dma((npos, steps)),
            dma((nt // PAIR,)), dma((nw // PAIR,)), dma((nc // PAIR,)), dma, dma((2,)), dma,
        ],
        compiler_params=pltpu.CompilerParams(
            collective_id=0, has_side_effects=True, vmem_limit_bytes=56 * 1024 * 1024
        ),
    )(active_adapter_owner, request_slot_index[:, :, 0], states, down_weights, up_weights)


def routed(n, cols, states, request_slot_index, down_weights, up_weights, active_adapter_owner):
    steps, rows, width = states.shape
    cap = 2 * rows // cols
    paired = steps == 2 and cap == 8 and cols * cap == down_weights.shape[1]
    if n == 4 and paired and width % (8 * WIDTH) == 0:
        run = functools.partial(split_body, cols)
    else:
        run = functools.partial(body, n, cols)
    return run(states, request_slot_index, down_weights, up_weights, active_adapter_owner)


def solution(mesh):
    return jax.shard_map(
        functools.partial(routed, mesh.shape["dp"], mesh.shape["adapter"]),
        mesh=mesh,
        in_specs=(
            P(None, ("dp", "adapter"), None),
            P(None, ("dp", "adapter"), None),
            P(("dp", "adapter"), None, None),
            P(("dp", "adapter"), None, None),
            P(),
        ),
        out_specs=P(None, ("dp", "adapter"), None),
        check_vma=False,
    )
```
